128 devices in a mesh: row: 16 (over x, y_hi, core), col: 8 (over z, y_lo).
Axes of the slice: x: 4, y: 4 (y_hi: 2, y_lo: 2; y = y_hi * 2 + y_lo), z: 4, core: 2. Of those that a mesh axis runs over, the one named last changes fastest.
Arguments:
- node_features: bfloat16 [32768, 512], P(('col', 'row')), may hold values from -6 to 6
- tile_values: bfloat16 [16, 1536, 128, 128], P('row', 'col'), may hold values from -0.078125 to 0.078125
- tile_rows: int32 [16, 1536], P('row', 'col'), may hold values from 0 to 15, as said below
- tile_cols: int32 [16, 1536], P('row', 'col'), may hold values from 0 to 31, as said below
- tile_count: int32 [16, 8], P('row', 'col'), may hold values from 3 to 192, as said below
- weight: bfloat16 [512, 512], replicated, may hold values from -0.25 to 0.25
- bias: float32 [512], replicated, may hold values from -3 to 3
- cotangent: bfloat16 [32768, 512], P(('row', 'col')), may hold values from -6 to 6
Outputs:
- output: bfloat16 [32768, 512], P(('row', 'col'))
- feature_grad: bfloat16 [32768, 512], P(('col', 'row'))
- weight_grad: float32 [512, 512], replicated
- bias_grad: float32 [512], replicated
The draws below stay inside these ranges and needn't reach their ends.
Inputs may be any that keep to these rules, and one draw needn't show every extreme that they name: `tile_rows`: within one grid block the used slots name distinct tiles; together with tile_cols each slot names one tile of the block. `tile_cols`: within one grid block the used slots name distinct tiles. `tile_count`: some grid block uses all 192 slots.
All inputs are finite; a program needn't handle non-finite values.
Results may differ from the reference program's by a relative error of at most 0.014.
Values may be sent and summed in bfloat16 or wider, within the bound.
No kernel may reach another device: no remote copies, remote signals or barrier semaphores. Data moves between devices by JAX's collectives and lax.ppermute only.
A program may use at most 128 MiB of HBM per device.

```python
import jax
import jax.numpy as jnp
from jax import lax

F = 512
TILE = 128
RT = 16
CT = 32
TMAX = 192
NODES = 32768
N_ROW = 16
N_COL = 8


def tile_slots(key):
    block_keys = jax.random.split(jax.random.fold_in(key, 11), N_ROW * N_COL)

    def pick_slots(block_key):
        return jax.random.permutation(block_key, RT * CT)[:TMAX]
    slots = jax.vmap(pick_slots)(block_keys)
    return slots.reshape(N_ROW, N_COL * TMAX).astype(jnp.int32)


def draw_tile_rows(key, part):
    return (tile_slots(key) // CT).astype(jnp.int32)


def draw_tile_cols(key, part):
    return (tile_slots(key) % CT).astype(jnp.int32)


def draw_tile_count(key, part):
    levels = jax.random.randint(jax.random.fold_in(key, 23), (N_ROW * N_COL,), 1, 9)
    busiest = jax.random.randint(jax.random.fold_in(key, 29), (), 0, N_ROW * N_COL)
    levels = jnp.where(jnp.arange(N_ROW * N_COL) == busiest, 8, levels)
    totals = jnp.maximum(1, TMAX * levels * levels // 64)
    return totals.reshape(N_ROW, N_COL).astype(jnp.int32)


def block_scale(stream_key, dims, cuts, low, high):
    def one(dim, blocks):
        draws = jax.random.uniform(jax.random.fold_in(jax.random.fold_in(stream_key, 6), dim), (blocks,), jnp.float32, low / len(cuts), high / len(cuts))
        return jnp.repeat(jnp.exp(draws), dims[dim] // blocks).reshape((-1,) + (1,) * (len(dims) - dim - 1))

    factor_of = one(*cuts[0])
    for cut in cuts[1:]:
        factor_of = factor_of * one(*cut)
    return factor_of


def centred(key, shape, scale, most, cuts=(), kind=jnp.bfloat16):
    result = scale * jax.random.normal(key, shape, jnp.float32)
    if cuts:
        result = result * block_scale(key, shape, cuts, -0.22, 0.18)
    return jnp.clip(result, -most, most).astype(kind)


def setup_inputs(seed: int = 0) -> dict:
    key_list = jax.random.split(jax.random.key(seed), 9)
    node_features = centred(key_list[0], (NODES, F), 1.0, 6.0, ((0, 128),))
    tile_values = centred(key_list[1], (N_ROW, N_COL * TMAX, TILE, TILE), (TILE * N_COL * TMAX // (2 * RT)) ** -0.5, 0.078125, ((0, 16), (1, 8)))
    tile_rows = draw_tile_rows(jax.random.fold_in(key_list[8], 71), 0)
    tile_cols = draw_tile_cols(jax.random.fold_in(key_list[8], 71), 0)
    tile_count = draw_tile_count(jax.random.fold_in(key_list[8], 71), 0)
    weight = centred(key_list[5], (F, F), F ** -0.5, 0.25)
    bias = centred(key_list[6], (F,), 0.5, 3.0, (), jnp.float32)
    cotangent = centred(key_list[7], (NODES, F), 1.0, 6.0, ((0, 128),))
    return {"node_features": node_features, "tile_values": tile_values, "tile_rows": tile_rows, "tile_cols": tile_cols, "tile_count": tile_count, "weight": weight, "bias": bias, "cotangent": cotangent}


def block_matrix(values, row_index, col_index, tile_total):
    in_range = jnp.arange(TMAX) < tile_total
    masked = jnp.where(in_range[:, None, None], values.astype(jnp.float32), jnp.float32(0.0))
    layout = jnp.zeros((RT, CT, TILE, TILE), jnp.float32).at[row_index, col_index].add(masked)
    return layout.transpose(0, 2, 1, 3).reshape(RT * TILE, CT * TILE)

def reference(node_features, tile_values, tile_rows, tile_cols, tile_count, weight, bias, cotangent):
    highest = lax.Precision.HIGHEST
    values_all = tile_values.reshape(N_ROW, N_COL, TMAX, TILE, TILE)
    rows_all = tile_rows.reshape(N_ROW, N_COL, TMAX)
    cols_all = tile_cols.reshape(N_ROW, N_COL, TMAX)
    column_blocks = node_features.astype(jnp.float32).reshape(N_COL, CT * TILE, F)

    def forward_block(row_block):
        running = jnp.zeros((RT * TILE, F), jnp.float32)
        for column in range(N_COL):
            matrix = block_matrix(values_all[row_block, column], rows_all[row_block, column], cols_all[row_block, column], tile_count[row_block, column])
            running = running + jnp.dot(matrix, column_blocks[column], precision=highest)
        return running
    summed = lax.map(forward_block, jnp.arange(N_ROW, dtype=jnp.int32))
    aggregated = summed.reshape(NODES, F).astype(jnp.bfloat16)
    pre_act = jnp.dot(aggregated, weight, preferred_element_type=jnp.float32) + bias
    sigmoid_pre = jax.nn.sigmoid(pre_act)
    output = (pre_act * sigmoid_pre).astype(jnp.bfloat16)
    grad_pre = (cotangent.astype(jnp.float32) * sigmoid_pre * (1.0 + pre_act * (1.0 - sigmoid_pre))).astype(jnp.bfloat16)
    grad_scale = 1.0 / jnp.sqrt(jnp.float32(NODES))
    weight_grad = jnp.dot(aggregated.T, grad_pre, preferred_element_type=jnp.float32) * grad_scale
    bias_grad = lax.optimization_barrier(jnp.sum(grad_pre.astype(jnp.float32), axis=0)) * grad_scale
    grad_rows = jnp.dot(grad_pre, weight.T, preferred_element_type=jnp.float32).astype(jnp.bfloat16)
    row_blocks = grad_rows.astype(jnp.float32).reshape(N_ROW, RT * TILE, F)

    def backward_block(column):
        running = jnp.zeros((CT * TILE, F), jnp.float32)
        for row_block in range(N_ROW):
            matrix = block_matrix(values_all[row_block, column], rows_all[row_block, column], cols_all[row_block, column], tile_count[row_block, column])
            running = running + jnp.dot(matrix.T, row_blocks[row_block], precision=highest)
        return running
    column_sums = lax.map(backward_block, jnp.arange(N_COL, dtype=jnp.int32))
    feature_grad = column_sums.reshape(NODES, F).astype(jnp.bfloat16)
    return (output, feature_grad, weight_grad, bias_grad)
```

```python
import math

import jax
import jax.numpy as jnp
from jax import lax
from jax.experimental import pallas as pl
from jax.experimental.pallas import tpu as pltpu
from jax.sharding import PartitionSpec as P


def dense_block(blocks, row_index, col_index, tile_total, row_tiles, col_tiles):
    slots, tile, _ = blocks.shape
    cells = row_tiles * col_tiles

    def kernel(rows_ref, cols_ref, total_ref, blocks_ref, out_ref, slot_of):
        strip = pl.program_id(0)

        @pl.when(strip == 0)
        def _():
            def clear(cell, carry):
                slot_of[cell] = -1
                return carry

            lax.fori_loop(0, cells, clear, 0, unroll=8)

            def mark(slot, carry):
                slot_of[rows_ref[slot] * col_tiles + cols_ref[slot]] = slot
                return carry

            lax.fori_loop(0, total_ref[0], mark, 0)

        for column in range(col_tiles):
            slot = slot_of[strip * col_tiles + column]
            value = blocks_ref[jnp.maximum(slot, 0)]
            out_ref[:, column * tile : (column + 1) * tile] = jnp.where(
                slot >= 0, value, jnp.zeros_like(value)
            )

    return pl.pallas_call(
        kernel,
        out_shape=jax.ShapeDtypeStruct((row_tiles * tile, col_tiles * tile), blocks.dtype),
        grid_spec=pltpu.PrefetchScalarGridSpec(
            num_scalar_prefetch=3,
            grid=(row_tiles,),
            in_specs=[
                pl.BlockSpec((slots, tile, tile), lambda i, *_: (0, 0, 0), pipeline_mode=pl.Buffered(1))
            ],
            out_specs=pl.BlockSpec((tile, col_tiles * tile), lambda i, *_: (i, 0)),
            scratch_shapes=[pltpu.SMEM((cells,), jnp.int32)],
        ),
        compiler_params=pltpu.CompilerParams(vmem_limit_bytes=24 * 1024 * 1024),
        cost_estimate=pl.CostEstimate(
            flops=0,
            bytes_accessed=2 * (blocks.size + cells * tile * tile),
            transcendentals=0,
        ),
        name="dense_block",
    )(row_index, col_index, tile_total, blocks)


def per_device(
    node_features, tile_values, tile_rows, tile_cols, tile_count, weight, bias, cotangent
):
    blocks = tile_values[0]
    tile = blocks.shape[-1]
    local_nodes = node_features.shape[0]
    row_tiles = local_nodes * lax.axis_size("col") // tile
    col_tiles = local_nodes * lax.axis_size("row") // tile
    node_total = local_nodes * lax.axis_size("row") * lax.axis_size("col")
    contract = (((0,), (0,)), ((), ()))
    back_form = (((1,), (1,)), ((), ()))

    matrix = dense_block(
        blocks, tile_rows[0], tile_cols[0], tile_count[0], row_tiles, col_tiles
    )
    node_panel = lax.all_gather(node_features, "row", axis=0, tiled=True)
    partial_value = jnp.dot(matrix, node_panel, preferred_element_type=jnp.float32).astype(
        jnp.bfloat16
    )
    aggregated = lax.psum_scatter(partial_value, "col", scatter_dimension=0, tiled=True)
    pre_act = jnp.dot(aggregated, weight, preferred_element_type=jnp.float32) + bias
    sigmoid_pre = jax.nn.sigmoid(pre_act)
    output = (pre_act * sigmoid_pre).astype(jnp.bfloat16)
    grad_pre = (
        cotangent.astype(jnp.float32) * sigmoid_pre * (1.0 + pre_act * (1.0 - sigmoid_pre))
    ).astype(jnp.bfloat16)
    local_grads = lax.dot_general(
        grad_pre, weight, back_form, preferred_element_type=jnp.float32
    ).astype(jnp.bfloat16)
    row_grads = lax.all_gather(local_grads, "col", axis=0, tiled=True)
    weight_local = lax.dot_general(
        aggregated, grad_pre, contract, preferred_element_type=jnp.float32
    )
    bias_local = jnp.sum(grad_pre.astype(jnp.float32), axis=0, keepdims=True)
    sums = lax.psum(
        jnp.concatenate([weight_local, jnp.broadcast_to(bias_local, (8, bias_local.shape[1]))], 0),
        ("row", "col"),
    )
    grad_scale = 1.0 / math.sqrt(node_total)
    column_partial = lax.dot_general(
        matrix, row_grads, contract, preferred_element_type=jnp.float32
    ).astype(jnp.bfloat16)
    feature_grad = lax.psum_scatter(column_partial, "row", scatter_dimension=0, tiled=True)
    width = weight_local.shape[0]
    return (output, feature_grad, sums[:width] * grad_scale, sums[width] * grad_scale)


def solution(mesh):
    return jax.shard_map(
        per_device,
        mesh=mesh,
        in_specs=(
            P(("col", "row"), None),
            P("row", "col", None, None),
            P("row", "col"),
            P("row", "col"),
            P("row", "col"),
            P(),
            P(),
            P(("row", "col"), None),
        ),
        out_specs=(P(("row", "col"), None), P(("col", "row"), None), P(), P()),
        check_vma=False,
    )
```

```python
import math

import jax
import jax.numpy as jnp
from jax import lax
from jax.experimental import pallas as pl
from jax.experimental.pallas import tpu as pltpu
from jax.sharding import Mesh, PartitionSpec as P


MIB = 1024 * 1024
STEPS = ((2, 1), (1, 1), (3, 1), (2, 0), (0, 1), (1, 0), (3, 0), (0, 0))
FAR = 3
ROW_CHIPS = ("x", "yh")
COL_CHIPS = ("z", "yl")
ALL_CHIPS = ROW_CHIPS + COL_CHIPS
HBM = pl.BlockSpec(memory_space=pl.ANY)


def send(value, axes, step):
    far, near = step
    pairs = [
        (a * 2 + b, ((a + far) % 4) * 2 + (b ^ near)) for a in range(4) for b in range(2)
    ]
    return lax.ppermute(value, axes, pairs)


def swap_cores(value):
    return lax.ppermute(value, "core", [(0, 1), (1, 0)])


def back(step):
    return ((4 - step[0]) % 4, step[1])


def place(first, second, first_here, second_here):
    code = ((first - first_here + 4) % 4) * 2 + (second ^ second_here)
    position = jnp.zeros_like(code)
    for index, (far, near) in enumerate(STEPS):
        position = jnp.where(code == far * 2 + near, index, position)
    return position


def dense_block(blocks, row_index, col_index, tile_total, row_tiles, col_tiles):
    slots, tile, _ = blocks.shape
    cells = row_tiles * col_tiles

    def kernel(rows_ref, cols_ref, total_ref, blocks_ref, out_ref, slot_of):
        strip = pl.program_id(0)

        @pl.when(strip == 0)
        def _():
            def clear(cell, carry):
                slot_of[cell] = -1
                return carry

            lax.fori_loop(0, cells, clear, 0, unroll=8)

            def mark(slot, carry):
                slot_of[rows_ref[slot] * col_tiles + cols_ref[slot]] = slot
                return carry

            lax.fori_loop(0, total_ref[0], mark, 0)

        for column in range(col_tiles):
            slot = slot_of[strip * col_tiles + column]
            value = blocks_ref[jnp.maximum(slot, 0)]
            out_ref[:, column * tile : (column + 1) * tile] = jnp.where(
                slot >= 0, value, jnp.zeros_like(value)
            )

    return pl.pallas_call(
        kernel,
        out_shape=jax.ShapeDtypeStruct((row_tiles * tile, col_tiles * tile), blocks.dtype),
        grid_spec=pltpu.PrefetchScalarGridSpec(
            num_scalar_prefetch=3,
            grid=(row_tiles,),
            in_specs=[
                pl.BlockSpec(
                    (slots, tile, tile), lambda i, *_: (0, 0, 0), pipeline_mode=pl.Buffered(1)
                )
            ],
            out_specs=pl.BlockSpec((tile, col_tiles * tile), lambda i, *_: (i, 0)),
            scratch_shapes=[pltpu.SMEM((cells,), jnp.int32)],
        ),
        compiler_params=pltpu.CompilerParams(vmem_limit_bytes=24 * MIB),
        cost_estimate=pl.CostEstimate(
            flops=0,
            bytes_accessed=2 * (blocks.size + cells * tile * tile),
            transcendentals=0,
        ),
        name="dense_block",
    )(row_index, col_index, tile_total, blocks)


def forward_products(matrix, shards, first, count):
    height, features = shards[0].shape
    depth = matrix.shape[1]
    parts = len(shards)

    def kernel(*refs):
        m_ref, x_refs, o_refs = refs[0], refs[1 : 1 + parts], refs[1 + parts : 1 + parts + count]
        m_buf, x_buf, o_buf, m_sem, x_sem, o_sem = refs[1 + parts + count :]

        def m_copy(block):
            rows = pl.ds(pl.multiple_of((first + block) * height, height), height)
            return pltpu.make_async_copy(m_ref.at[rows], m_buf.at[block], m_sem.at[block])

        def x_copy(part):
            return pltpu.make_async_copy(
                x_refs[part], x_buf.at[pl.ds(part * height, height)], x_sem.at[part]
            )

        def o_copy(block):
            return pltpu.make_async_copy(o_buf.at[block], o_refs[block], o_sem.at[block])

        m_copy(0).start()
        for part in range(parts):
            x_copy(part).start()
        for block in range(1, count):
            m_copy(block).start()
        for part in range(parts):
            x_copy(part).wait()

        @pl.loop(0, count)
        def _(block):
            m_copy(block).wait()
            o_buf[block] = jnp.dot(
                m_buf[block], x_buf[...], preferred_element_type=jnp.float32
            ).astype(o_buf.dtype)
            for index in range(count):

                @pl.when(block == index)
                def _():
                    o_copy(index).start()

        for block in range(count):
            o_copy(block).wait()

    return pl.pallas_call(
        kernel,
        out_shape=[jax.ShapeDtypeStruct((height, features), jnp.bfloat16)] * count,
        in_specs=[HBM] * (1 + parts),
        out_specs=[HBM] * count,
        scratch_shapes=[
            pltpu.VMEM((count, height, depth), matrix.dtype),
            pltpu.VMEM((depth, features), jnp.bfloat16),
            pltpu.VMEM((count, height, features), jnp.bfloat16),
            pltpu.SemaphoreType.DMA((count,)),
            pltpu.SemaphoreType.DMA((parts,)),
            pltpu.SemaphoreType.DMA((count,)),
        ],
        compiler_params=pltpu.CompilerParams(vmem_limit_bytes=32 * MIB),
        cost_estimate=pl.CostEstimate(
            flops=2 * count * height * depth * features,
            bytes_accessed=2 * (count * height * (depth + features) + depth * features),
            transcendentals=0,
        ),
        name="forward_products",
    )(matrix, *shards)


def backward_products(matrix, grads, first, count, carried, split):
    features, width = grads[0].shape
    depth = matrix.shape[0]
    parts = len(grads)
    carries = 0 if carried is None else 1
    outs = count if split else 1

    def kernel(*refs):
        m_ref, g_refs = refs[0], refs[1 : 1 + parts]
        c_refs = refs[1 + parts : 1 + parts + carries]
        o_refs = refs[1 + parts + carries : 1 + parts + carries + outs]
        rest = refs[1 + parts + carries + outs :]
        m_buf, g_buf, o_buf, m_sem, g_sem, o_sem = rest[:6]
        c_buf, c_sem = rest[6:] if carries else (None, None)

        def m_copy(block):
            columns = pl.ds(pl.multiple_of((first + block) * width, width), width)
            return pltpu.make_async_copy(m_ref.at[:, columns], m_buf.at[block], m_sem.at[block])

        def g_copy(part):
            return pltpu.make_async_copy(
                g_refs[part], g_buf.at[:, pl.ds(part * width, width)], g_sem.at[part]
            )

        def c_copy(block):
            return pltpu.make_async_copy(
                c_refs[0].at[:, pl.ds(pl.multiple_of(block * width, width), width)],
                c_buf.at[block],
                c_sem.at[block],
            )

        def o_copy(block):
            target = o_refs[block] if split else o_refs[0].at[:, pl.ds(block * width, width)]
            return pltpu.make_async_copy(o_buf.at[block], target, o_sem.at[block])

        m_copy(0).start()
        for part in range(parts):
            g_copy(part).start()
        for block in range(count):
            if block:
                m_copy(block).start()
            if carries:
                c_copy(block).start()
        for part in range(parts):
            g_copy(part).wait()

        @pl.loop(0, count)
        def _(block):
            m_copy(block).wait()
            total = jnp.dot(g_buf[...], m_buf[block], preferred_element_type=jnp.float32)
            if carries:
                c_copy(block).wait()
                total = total + c_buf[block].astype(jnp.float32)
            o_buf[block] = total.astype(o_buf.dtype)
            for index in range(count):

                @pl.when(block == index)
                def _():
                    o_copy(index).start()

        for block in range(count):
            o_copy(block).wait()

    shape = (features, width) if split else (features, count * width)
    scratch = [
        pltpu.VMEM((count, depth, width), matrix.dtype),
        pltpu.VMEM((features, depth), jnp.bfloat16),
        pltpu.VMEM((count, features, width), jnp.bfloat16),
        pltpu.SemaphoreType.DMA((count,)),
        pltpu.SemaphoreType.DMA((parts,)),
        pltpu.SemaphoreType.DMA((count,)),
    ]
    if carries:
        scratch += [
            pltpu.VMEM((count, features, width), jnp.bfloat16),
            pltpu.SemaphoreType.DMA((count,)),
        ]
    return pl.pallas_call(
        kernel,
        out_shape=[jax.ShapeDtypeStruct(shape, jnp.bfloat16)] * outs,
        in_specs=[HBM] * (1 + parts + carries),
        out_specs=[HBM] * outs,
        scratch_shapes=scratch,
        compiler_params=pltpu.CompilerParams(vmem_limit_bytes=32 * MIB),
        cost_estimate=pl.CostEstimate(
            flops=2 * count * width * depth * features,
            bytes_accessed=2 * (count * width * (depth + features) + depth * features),
            transcendentals=0,
        ),
        name="backward_products",
    )(matrix, *grads, *(() if carried is None else (carried,)))


def node_layer(terms, weight, bias, cotangent):
    nodes, features = cotangent.shape
    parts = len(terms)

    def kernel(*refs):
        term_refs = refs[:parts]
        weight_ref, bias_ref, cotangent_ref = refs[parts : parts + 3]
        output_ref, aggregated_ref, grad_pre_ref, grads_ref = refs[parts + 3 :]
        total = term_refs[0][...].astype(jnp.float32)
        for ref in term_refs[1:]:
            total = total + ref[...].astype(jnp.float32)
        aggregated = total.astype(jnp.bfloat16)
        aggregated_ref[...] = aggregated
        pre = (
            jnp.dot(aggregated, weight_ref[...], preferred_element_type=jnp.float32)
            + bias_ref[...]
        )
        gate = jax.nn.sigmoid(pre)
        output_ref[...] = (pre * gate).astype(jnp.bfloat16)
        grad_pre = (
            cotangent_ref[...].astype(jnp.float32) * gate * (1.0 + pre * (1.0 - gate))
        ).astype(jnp.bfloat16)
        grad_pre_ref[...] = grad_pre
        grads_ref[...] = lax.dot_general(
            weight_ref[...],
            grad_pre,
            (((1,), (1,)), ((), ())),
            preferred_element_type=jnp.float32,
        ).astype(jnp.bfloat16)

    same = jax.ShapeDtypeStruct((nodes, features), jnp.bfloat16)
    return pl.pallas_call(
        kernel,
        out_shape=[same, same, same, jax.ShapeDtypeStruct((features, nodes), jnp.bfloat16)],
        compiler_params=pltpu.CompilerParams(vmem_limit_bytes=24 * MIB),
        cost_estimate=pl.CostEstimate(
            flops=4 * nodes * features * features,
            bytes_accessed=2 * (12 * nodes * features + features * features),
            transcendentals=nodes * features,
        ),
        name="node_layer",
    )(*terms, weight, bias.reshape(1, features), cotangent)


def transposed_sum(terms):
    features, nodes = terms[0].shape

    def kernel(*refs):
        total = refs[0][...].astype(jnp.float32)
        for ref in refs[1:-1]:
            total = total + ref[...].astype(jnp.float32)
        refs[-1][...] = total.T.astype(jnp.bfloat16)

    return pl.pallas_call(
        kernel,
        out_shape=jax.ShapeDtypeStruct((nodes, features), jnp.bfloat16),
        compiler_params=pltpu.CompilerParams(vmem_limit_bytes=24 * MIB),
        name="transposed_sum",
    )(*terms)


def sum_over_devices(weight_local, bias_local):
    core = lax.axis_index("core")
    height, features = weight_local.shape
    half = height // 2
    chips = lax.axis_size(ALL_CHIPS)
    mine = lax.dynamic_slice_in_dim(weight_local, core * half, half, 0)
    other = lax.dynamic_slice_in_dim(weight_local, (1 - core) * half, half, 0)
    mine = mine + swap_cores(other)
    rows = half // chips
    payload = jnp.concatenate(
        [
            mine.reshape(chips, rows, features),
            jnp.broadcast_to(bias_local.reshape(1, rows, features // rows), (chips, rows, features // rows)),
        ],
        axis=2,
    )
    totals = jnp.sum(lax.all_to_all(payload, ALL_CHIPS, 0, 0, tiled=True), axis=0)
    spread = jnp.broadcast_to(totals[None, :, :features], (chips, rows, features))
    half_sum = lax.all_to_all(spread, ALL_CHIPS, 0, 0, tiled=True).reshape(half, features)
    bias_half = totals[:, features:].reshape(1, features)
    packed = jnp.concatenate([half_sum, jnp.broadcast_to(bias_half, (8, features))], 0)
    theirs = swap_cores(packed)
    first = jnp.where(core == 0, half_sum, theirs[:half])
    second = jnp.where(core == 0, theirs[:half], half_sum)
    return jnp.concatenate([first, second], 0), (bias_half + theirs[half : half + 1])[0]


def per_device(
    node_features, tile_values, tile_rows, tile_cols, tile_count, weight, bias, cotangent
):
    blocks = tile_values[0]
    tile = blocks.shape[-1]
    local_nodes = node_features.shape[0]
    step_tiles = local_nodes // tile
    row_tiles = step_tiles * lax.axis_size(COL_CHIPS)
    col_tiles = step_tiles * lax.axis_size(ROW_CHIPS + ("core",))
    node_total = local_nodes * lax.axis_size(ALL_CHIPS + ("core",))
    x, yh, core = lax.axis_index("x"), lax.axis_index("yh"), lax.axis_index("core")
    z, yl = lax.axis_index("z"), lax.axis_index("yl")
    steps = len(STEPS)

    owner = tile_rows[0] // step_tiles
    row_place = place(owner // 2, owner % 2, z, yl) * step_tiles + tile_rows[0] % step_tiles
    owner = tile_cols[0] // step_tiles
    col_place = place(owner // 4, (owner // 2) % 2, x, yh) + steps * ((owner % 2) ^ core)
    col_place = col_place * step_tiles + tile_cols[0] % step_tiles
    matrix = dense_block(blocks, row_place, col_place, tile_count[0], row_tiles, col_tiles)

    own = [send(node_features, ROW_CHIPS, back(step)) for step in STEPS[:-1]] + [node_features]
    shards = own + [swap_cores(shard) for shard in own]

    partials = forward_products(matrix, shards, 0, FAR)
    arrived = [send(p, COL_CHIPS, s) for p, s in zip(partials, STEPS)]
    rest = forward_products(matrix, shards, FAR, steps - FAR)
    arrived += [send(p, COL_CHIPS, s) for p, s in zip(rest[:-1], STEPS[FAR:])]
    output, aggregated, grad_pre, grads = node_layer(
        [rest[-1]] + arrived, weight, bias, cotangent
    )

    all_grads = [send(grads, COL_CHIPS, back(step)) for step in STEPS[:-1]] + [grads]
    weight_local = lax.dot_general(
        aggregated, grad_pre, (((0,), (0,)), ((), ())), preferred_element_type=jnp.float32
    )
    bias_local = jnp.sum(grad_pre.astype(jnp.float32), axis=0)
    weight_sum, bias_sum = sum_over_devices(weight_local, bias_local)

    (far_out,) = backward_products(matrix, all_grads, steps, FAR, None, False)
    far_in = swap_cores(far_out)
    (near_out,) = backward_products(matrix, all_grads, steps + FAR, steps - FAR, None, False)
    near_in = swap_cores(near_out)
    partials = backward_products(matrix, all_grads, 0, FAR, far_in, True)
    arrived = [send(p, ROW_CHIPS, s) for p, s in zip(partials, STEPS)]
    rest = backward_products(matrix, all_grads, FAR, steps - FAR, near_in, True)
    arrived += [send(p, ROW_CHIPS, s) for p, s in zip(rest[:-1], STEPS[FAR:])]
    feature_grad = transposed_sum([rest[-1]] + arrived)

    grad_scale = 1.0 / math.sqrt(node_total)
    return (output, feature_grad, weight_sum * grad_scale, bias_sum * grad_scale)


def solution(mesh):
    mesh = Mesh(mesh.devices.reshape(4, 2, 2, 4, 2), ("x", "yh", "core", "z", "yl"))
    row, col = ("x", "yh", "core"), ("z", "yl")
    return jax.shard_map(
        per_device,
        mesh=mesh,
        in_specs=(
            P(col + row, None),
            P(row, col, None, None),
            P(row, col),
            P(row, col),
            P(row, col),
            P(),
            P(),
            P(row + col, None),
        ),
        out_specs=(P(row + col, None), P(col + row, None), P(), P()),
        check_vma=False,
    )
```

```python
import math

import jax
import jax.numpy as jnp
from jax import lax
from jax.experimental import pallas as pl
from jax.experimental.pallas import tpu as pltpu
from jax.sharding import Mesh, PartitionSpec as P


STEPS = ((2, 1), (1, 1), (3, 1), (2, 0), (0, 1), (1, 0), (3, 0), (0, 0))
FAR = 4
ROW_CHIPS = ("x", "yh")
COL_CHIPS = ("z", "yl")
ALL_CHIPS = ROW_CHIPS + COL_CHIPS
GRANT = 32 * 1024 * 1024
PLANES = 3
HBM = pl.BlockSpec(memory_space=pltpu.HBM)
ANY = pl.BlockSpec(memory_space=pl.ANY)


def send(value, axes, step):
    far, near = step
    pairs = [
        (a * 2 + b, ((a + far) % 4) * 2 + (b ^ near)) for a in range(4) for b in range(2)
    ]
    return lax.ppermute(value, axes, pairs)


def swap_cores(value):
    return lax.ppermute(value, "core", [(0, 1), (1, 0)])


def back(step):
    return ((4 - step[0]) % 4, step[1])


def place(first, second, first_here, second_here):
    code = ((first - first_here + 4) % 4) * 2 + (second ^ second_here)
    position = jnp.zeros_like(code)
    for index, (far, near) in enumerate(STEPS):
        position = jnp.where(code == far * 2 + near, index, position)
    return position


def dense_block(blocks, row_index, col_index, tile_total, row_tiles, col_tiles):
    slots, tile, _ = blocks.shape
    cells = row_tiles * col_tiles

    def kernel(rows_ref, cols_ref, total_ref, blocks_ref, out_ref, slot_of, tiles, strips, t_sem, s_sem):
        load = pltpu.make_async_copy(blocks_ref, tiles, t_sem)
        load.start()

        def clear(cell, carry):
            slot_of[cell] = -1
            return carry

        lax.fori_loop(0, cells, clear, 0, unroll=8)

        def mark(slot, carry):
            slot_of[rows_ref[slot] * col_tiles + cols_ref[slot]] = slot
            return carry

        lax.fori_loop(0, total_ref[0], mark, 0)
        load.wait()

        def store(strip, side):
            rows = pl.ds(pl.multiple_of(strip * tile, tile), tile)
            return pltpu.make_async_copy(strips.at[side], out_ref.at[0, rows], s_sem.at[side])

        @pl.loop(0, row_tiles // 2)
        def _(pair):
            for side in range(2):
                strip = pair * 2 + side

                @pl.when(pair > 0)
                def _():
                    store(strip - 2, side).wait()

                for column in range(col_tiles):
                    slot = slot_of[strip * col_tiles + column]
                    value = tiles[jnp.maximum(slot, 0)]
                    strips[side, :, column * tile : (column + 1) * tile] = jnp.where(
                        slot >= 0, value, jnp.zeros_like(value)
                    )
                store(strip, side).start()

        for side in range(2):
            store(row_tiles - 2 + side, side).wait()

    smem = pl.BlockSpec(memory_space=pltpu.SMEM)
    return pl.pallas_call(
        kernel,
        out_shape=jax.ShapeDtypeStruct((PLANES, row_tiles * tile, col_tiles * tile), blocks.dtype),
        in_specs=[smem, smem, smem, HBM],
        out_specs=HBM,
        scratch_shapes=[
            pltpu.SMEM((cells,), jnp.int32),
            pltpu.VMEM((slots, tile, tile), blocks.dtype),
            pltpu.VMEM((2, tile, col_tiles * tile), blocks.dtype),
            pltpu.SemaphoreType.DMA,
            pltpu.SemaphoreType.DMA((2,)),
        ],
        compiler_params=pltpu.CompilerParams(vmem_limit_bytes=GRANT),
        cost_estimate=pl.CostEstimate(
            flops=0,
            bytes_accessed=2 * (blocks.size + cells * tile * tile),
            transcendentals=0,
        ),
        name="dense_block",
    )(row_index, col_index, tile_total, blocks)


def forward_products(matrix, shards, first, count):
    height, features = shards[0].shape
    depth = matrix.shape[2]
    parts = len(shards)

    def kernel(*refs):
        m_ref, x_refs, o_refs = refs[0], refs[1 : 1 + parts], refs[1 + parts : 1 + parts + count]
        m_buf, x_buf, o_buf, m_sem, x_sem, o_sem = refs[1 + parts + count :]

        def m_copy(block):
            rows = pl.ds(pl.multiple_of((first + block) * height, height), height)
            return pltpu.make_async_copy(m_ref.at[0, rows], m_buf.at[block], m_sem.at[block])

        def x_copy(part):
            return pltpu.make_async_copy(
                x_refs[part], x_buf.at[pl.ds(part * height, height)], x_sem.at[part]
            )

        def o_copy(block):
            return pltpu.make_async_copy(o_buf.at[block], o_refs[block], o_sem.at[block])

        m_copy(0).start()
        for part in range(parts):
            x_copy(part).start()
        for block in range(1, count):
            m_copy(block).start()
        for part in range(parts):
            x_copy(part).wait()

        @pl.loop(0, count)
        def _(block):
            m_copy(block).wait()
            o_buf[block] = jnp.dot(
                m_buf[block], x_buf[...], preferred_element_type=jnp.float32
            ).astype(o_buf.dtype)
            for index in range(count):

                @pl.when(block == index)
                def _():
                    o_copy(index).start()

        for block in range(count):
            o_copy(block).wait()

    return pl.pallas_call(
        kernel,
        out_shape=[jax.ShapeDtypeStruct((height, features), jnp.bfloat16)] * count,
        in_specs=[HBM] + [ANY] * parts,
        out_specs=[ANY] * count,
        scratch_shapes=[
            pltpu.VMEM((count, height, depth), matrix.dtype),
            pltpu.VMEM((depth, features), jnp.bfloat16),
            pltpu.VMEM((count, height, features), jnp.bfloat16),
            pltpu.SemaphoreType.DMA((count,)),
            pltpu.SemaphoreType.DMA((parts,)),
            pltpu.SemaphoreType.DMA((count,)),
        ],
        compiler_params=pltpu.CompilerParams(vmem_limit_bytes=GRANT),
        cost_estimate=pl.CostEstimate(
            flops=2 * count * height * depth * features,
            bytes_accessed=2 * (count * height * (depth + features) + depth * features),
            transcendentals=0,
        ),
        name="forward_products",
    )(matrix, *shards)


def backward_products(matrix, grads, first, count, carried, split):
    features, width = grads[0].shape
    depth = matrix.shape[1]
    parts = len(grads)
    carries = 0 if carried is None else 1
    outs = count if split else 1

    def kernel(*refs):
        m_ref, g_refs = refs[0], refs[1 : 1 + parts]
        c_refs = refs[1 + parts : 1 + parts + carries]
        o_refs = refs[1 + parts + carries : 1 + parts + carries + outs]
        rest = refs[1 + parts + carries + outs :]
        m_buf, g_buf, o_buf, m_sem, g_sem, o_sem = rest[:6]
        c_buf, c_sem = rest[6:] if carries else (None, None)

        def m_copy(block):
            columns = pl.ds(pl.multiple_of((first + block) * width, width), width)
            return pltpu.make_async_copy(m_ref.at[0, :, columns], m_buf.at[block], m_sem.at[block])

        def g_copy(part):
            return pltpu.make_async_copy(
                g_refs[part], g_buf.at[:, pl.ds(part * width, width)], g_sem.at[part]
            )

        def c_copy(block):
            return pltpu.make_async_copy(
                c_refs[0].at[:, pl.ds(pl.multiple_of(block * width, width), width)],
                c_buf.at[block],
                c_sem.at[block],
            )

        def o_copy(block):
            target = o_refs[block] if split else o_refs[0].at[:, pl.ds(block * width, width)]
            return pltpu.make_async_copy(o_buf.at[block], target, o_sem.at[block])

        m_copy(0).start()
        for part in range(parts):
            g_copy(part).start()
        for block in range(count):
            if block:
                m_copy(block).start()
            if carries:
                c_copy(block).start()
        for part in range(parts):
            g_copy(part).wait()

        @pl.loop(0, count)
        def _(block):
            m_copy(block).wait()
            total = jnp.dot(g_buf[...], m_buf[block], preferred_element_type=jnp.float32)
            if carries:
                c_copy(block).wait()
                total = total + c_buf[block].astype(jnp.float32)
            o_buf[block] = total.astype(o_buf.dtype)
            for index in range(count):

                @pl.when(block == index)
                def _():
                    o_copy(index).start()

        for block in range(count):
            o_copy(block).wait()

    shape = (features, width) if split else (features, count * width)
    scratch = [
        pltpu.VMEM((count, depth, width), matrix.dtype),
        pltpu.VMEM((features, depth), jnp.bfloat16),
        pltpu.VMEM((count, features, width), jnp.bfloat16),
        pltpu.SemaphoreType.DMA((count,)),
        pltpu.SemaphoreType.DMA((parts,)),
        pltpu.SemaphoreType.DMA((count,)),
    ]
    if carries:
        scratch += [
            pltpu.VMEM((count, features, width), jnp.bfloat16),
            pltpu.SemaphoreType.DMA((count,)),
        ]
    return pl.pallas_call(
        kernel,
        out_shape=[jax.ShapeDtypeStruct(shape, jnp.bfloat16)] * outs,
        in_specs=[HBM] + [ANY] * (parts + carries),
        out_specs=[ANY] * outs,
        scratch_shapes=scratch,
        compiler_params=pltpu.CompilerParams(vmem_limit_bytes=GRANT),
        cost_estimate=pl.CostEstimate(
            flops=2 * count * width * depth * features,
            bytes_accessed=2 * (count * width * (depth + features) + depth * features),
            transcendentals=0,
        ),
        name="backward_products",
    )(matrix, *grads, *(() if carried is None else (carried,)))


def load_all(sources, targets, sems):
    copies = [
        pltpu.make_async_copy(source, target, sems.at[index])
        for index, (source, target) in enumerate(zip(sources, targets))
    ]
    for copy in copies:
        copy.start()
    return copies


def node_layer(terms, weight, bias, cotangent):
    nodes, features = cotangent.shape
    parts = len(terms)

    def kernel(*refs):
        sources = refs[: parts + 3]
        output_ref, aggregated_ref, grad_pre_ref, grads_ref = refs[parts + 3 : parts + 7]
        t_buf, w_buf, b_buf, c_buf, sems = refs[parts + 7 :]
        targets = [t_buf.at[part] for part in range(parts)] + [w_buf, b_buf, c_buf]
        copies = load_all(sources, targets, sems)
        copies[0].wait()
        total = t_buf[0].astype(jnp.float32)
        for part in range(1, parts):
            copies[part].wait()
            total = total + t_buf[part].astype(jnp.float32)
        aggregated = total.astype(jnp.bfloat16)
        aggregated_ref[...] = aggregated
        for copy in copies[parts:]:
            copy.wait()
        pre = jnp.dot(aggregated, w_buf[...], preferred_element_type=jnp.float32) + b_buf[...]
        gate = jax.nn.sigmoid(pre)
        output_ref[...] = (pre * gate).astype(jnp.bfloat16)
        grad_pre = (
            c_buf[...].astype(jnp.float32) * gate * (1.0 + pre * (1.0 - gate))
        ).astype(jnp.bfloat16)
        grad_pre_ref[...] = grad_pre
        grads_ref[...] = lax.dot_general(
            w_buf[...],
            grad_pre,
            (((1,), (1,)), ((), ())),
            preferred_element_type=jnp.float32,
        ).astype(jnp.bfloat16)

    same = jax.ShapeDtypeStruct((nodes, features), jnp.bfloat16)
    return pl.pallas_call(
        kernel,
        out_shape=[same, same, same, jax.ShapeDtypeStruct((features, nodes), jnp.bfloat16)],
        in_specs=[ANY] * (parts + 3),
        scratch_shapes=[
            pltpu.VMEM((parts, nodes, features), jnp.bfloat16),
            pltpu.VMEM((features, features), jnp.bfloat16),
            pltpu.VMEM((1, features), jnp.float32),
            pltpu.VMEM((nodes, features), jnp.bfloat16),
            pltpu.SemaphoreType.DMA((parts + 3,)),
        ],
        compiler_params=pltpu.CompilerParams(vmem_limit_bytes=GRANT),
        cost_estimate=pl.CostEstimate(
            flops=4 * nodes * features * features,
            bytes_accessed=2 * (12 * nodes * features + features * features),
            transcendentals=nodes * features,
        ),
        name="node_layer",
    )(*terms, weight, bias.reshape(1, features), cotangent)


def transposed_sum(terms):
    features, nodes = terms[0].shape
    parts = len(terms)

    def kernel(*refs):
        out_ref, t_buf, sems = refs[parts:]
        copies = load_all(refs[:parts], [t_buf.at[part] for part in range(parts)], sems)
        copies[0].wait()
        total = t_buf[0].astype(jnp.float32)
        for part in range(1, parts):
            copies[part].wait()
            total = total + t_buf[part].astype(jnp.float32)
        out_ref[...] = total.T.astype(jnp.bfloat16)

    return pl.pallas_call(
        kernel,
        out_shape=jax.ShapeDtypeStruct((nodes, features), jnp.bfloat16),
        in_specs=[ANY] * parts,
        scratch_shapes=[
            pltpu.VMEM((parts, features, nodes), jnp.bfloat16),
            pltpu.SemaphoreType.DMA((parts,)),
        ],
        compiler_params=pltpu.CompilerParams(vmem_limit_bytes=GRANT),
        cost_estimate=pl.CostEstimate(
            flops=parts * nodes * features,
            bytes_accessed=2 * (parts + 1) * nodes * features,
            transcendentals=0,
        ),
        name="transposed_sum",
    )(*terms)


def scatter_weight_sums(weight_local, bias_local):
    core = lax.axis_index("core")
    height, features = weight_local.shape
    half = height // 2
    chips = lax.axis_size(ALL_CHIPS)
    mine = lax.dynamic_slice_in_dim(weight_local, core * half, half, 0)
    other = lax.dynamic_slice_in_dim(weight_local, (1 - core) * half, half, 0)
    mine = mine + swap_cores(other)
    rows = half // chips
    width = features // rows
    payload = jnp.concatenate(
        [
            mine.reshape(chips, rows, features),
            jnp.broadcast_to(bias_local.reshape(1, rows, width), (chips, rows, width)),
        ],
        axis=2,
    )
    parts = lax.all_to_all(payload, ALL_CHIPS, 0, 0, tiled=True)
    totals = jnp.sum(parts, axis=0)
    return totals[:, :features], totals[:, features:]


def gather_weight_sums(spread):
    return lax.all_to_all(spread, ("core",) + ALL_CHIPS, 0, 0, tiled=True)


def after(value, *others):
    return lax.optimization_barrier((value,) + others)[0]


def per_device(
    node_features, tile_values, tile_rows, tile_cols, tile_count, weight, bias, cotangent
):
    blocks = tile_values[0]
    tile = blocks.shape[-1]
    local_nodes = node_features.shape[0]
    step_tiles = local_nodes // tile
    row_tiles = step_tiles * lax.axis_size(COL_CHIPS)
    col_tiles = step_tiles * lax.axis_size(ROW_CHIPS + ("core",))
    node_total = local_nodes * lax.axis_size(ALL_CHIPS + ("core",))
    x, yh, core = lax.axis_index("x"), lax.axis_index("yh"), lax.axis_index("core")
    z, yl = lax.axis_index("z"), lax.axis_index("yl")
    steps = len(STEPS)

    owner = tile_rows[0] // step_tiles
    row_place = place(owner // 2, owner % 2, z, yl) * step_tiles + tile_rows[0] % step_tiles
    owner = tile_cols[0] // step_tiles
    col_place = place(owner // 4, (owner // 2) % 2, x, yh) + steps * ((owner % 2) ^ core)
    col_place = col_place * step_tiles + tile_cols[0] % step_tiles
    matrix = dense_block(blocks, row_place, col_place, tile_count[0], row_tiles, col_tiles)

    own = [send(node_features, ROW_CHIPS, back(step)) for step in STEPS[:-1]] + [node_features]
    *own, matrix = lax.optimization_barrier((*own, matrix))
    shards = own + [swap_cores(shard) for shard in own]

    partials = forward_products(matrix, shards, 0, FAR)
    arrived = [send(p, COL_CHIPS, s) for p, s in zip(partials, STEPS)]
    rest = forward_products(matrix, shards, FAR, steps - FAR)
    arrived += [send(p, COL_CHIPS, s) for p, s in zip(rest[:-1], STEPS[FAR:])]
    output, aggregated, grad_pre, grads = node_layer(
        [rest[-1]] + arrived, weight, bias, cotangent
    )

    all_grads = [send(grads, COL_CHIPS, back(step)) for step in STEPS[:-1]] + [grads]
    weight_local = lax.dot_general(
        aggregated, grad_pre, (((0,), (0,)), ((), ())), preferred_element_type=jnp.float32
    )
    bias_local = jnp.sum(grad_pre.astype(jnp.float32), axis=0)
    weight_rows, bias_half = scatter_weight_sums(weight_local, bias_local)

    (far_out,) = backward_products(matrix, all_grads, steps, FAR, None, False)
    far_in = swap_cores(far_out)
    partials = backward_products(matrix, all_grads, 0, FAR, far_in, True)
    arrived = [send(p, ROW_CHIPS, s) for p, s in zip(partials, STEPS)]
    spread = jnp.broadcast_to(
        after(weight_rows, partials[0])[None].astype(jnp.bfloat16),
        (node_total // local_nodes,) + weight_rows.shape,
    )
    weight_sum = gather_weight_sums(spread)
    near_grads = [after(all_grads[0], spread)] + all_grads[1:]
    (near_out,) = backward_products(matrix, near_grads, steps + FAR, steps - FAR, None, False)
    near_in = swap_cores(near_out)
    rest = backward_products(matrix, near_grads, FAR, steps - FAR, near_in, True)
    arrived += [send(p, ROW_CHIPS, s) for p, s in zip(rest[:-1], STEPS[FAR:])]
    feature_grad = transposed_sum([rest[-1]] + arrived)

    grad_scale = 1.0 / math.sqrt(node_total)
    weight_grad = weight_sum.astype(jnp.float32).reshape(weight.shape) * grad_scale
    bias_sum = (bias_half + swap_cores(bias_half)).reshape(bias.shape)
    return (output, feature_grad, weight_grad, bias_sum * grad_scale)


def solution(mesh):
    mesh = Mesh(mesh.devices.reshape(4, 2, 2, 4, 2), ("x", "yh", "core", "z", "yl"))
    row, col = ("x", "yh", "core"), ("z", "yl")
    return jax.shard_map(
        per_device,
        mesh=mesh,
        in_specs=(
            P(col + row, None),
            P(row, col, None, None),
            P(row, col),
            P(row, col),
            P(row, col),
            P(),
            P(),
            P(row + col, None),
        ),
        out_specs=(P(row + col, None), P(col + row, None), P(), P()),
        check_vma=False,
    )
```

```python
import math

import jax
import jax.numpy as jnp
from jax import lax
from jax.experimental import pallas as pl
from jax.experimental.pallas import tpu as pltpu
from jax.sharding import Mesh, PartitionSpec as P


LANES = 128
STEPS = ((2, 1), (1, 1), (3, 1), (2, 0), (0, 1), (1, 0), (3, 0), (0, 0))
FAR = 4
ROW_CHIPS = ("x", "yh")
COL_CHIPS = ("z", "yl")
ALL_CHIPS = ROW_CHIPS + COL_CHIPS
GRANT = 32 * 1024 * 1024
WIDE_GRANT = 58 * 1024 * 1024
PLANES = 3
ANY = pl.BlockSpec(memory_space=pl.ANY)


def send(value, axes, step):
    far, near = step
    pairs = [
        (a * 2 + b, ((a + far) % 4) * 2 + (b ^ near)) for a in range(4) for b in range(2)
    ]
    return lax.ppermute(value, axes, pairs)


def swap_cores(value):
    return lax.ppermute(value, "core", [(0, 1), (1, 0)])


def back(step):
    return ((4 - step[0]) % 4, step[1])


def place(first, second, first_here, second_here):
    code = ((first - first_here + 4) % 4) * 2 + (second ^ second_here)
    position = jnp.zeros_like(code)
    for index, (far, near) in enumerate(STEPS):
        position = jnp.where(code == far * 2 + near, index, position)
    return position


def dense_block(blocks, row_index, col_index, tile_total, row_tiles, col_tiles):
    slots, tile, _ = blocks.shape
    height, width = row_tiles * tile, col_tiles * tile
    loads, stores, fill = 4, 8, 32
    share = slots // loads

    def kernel(rows_ref, cols_ref, total_ref, blocks_ref, out_ref, tiles, image, t_sem, s_sem):
        def load(part):
            span = pl.ds(part * share, share)
            return pltpu.make_async_copy(blocks_ref.at[span], tiles.at[span], t_sem.at[part])

        def store(part):
            span = pl.ds(part * (height // stores), height // stores)
            return pltpu.make_async_copy(image.at[span], out_ref.at[0, span], s_sem.at[part])

        for part in range(loads):
            load(part).start()

        @pl.loop(0, height // fill)
        def _(index):
            image[pl.ds(pl.multiple_of(index * fill, fill), fill)] = jnp.zeros(
                (fill, width), image.dtype
            )

        total = total_ref[0]
        for part in range(loads):
            load(part).wait()

            def put(slot, carry):
                rows = pl.ds(pl.multiple_of(rows_ref[slot] * tile, tile), tile)
                cols = pl.ds(pl.multiple_of(cols_ref[slot] * tile, tile), tile)
                image[rows, cols] = tiles[slot]
                return carry

            lax.fori_loop(part * share, jnp.minimum((part + 1) * share, total), put, 0)
        for part in range(stores):
            store(part).start()
        for part in range(stores):
            store(part).wait()

    smem = pl.BlockSpec(memory_space=pltpu.SMEM)
    return pl.pallas_call(
        kernel,
        out_shape=jax.ShapeDtypeStruct((PLANES, height, width), blocks.dtype),
        in_specs=[smem, smem, smem, ANY],
        out_specs=ANY,
        scratch_shapes=[
            pltpu.VMEM((slots, tile, tile), blocks.dtype),
            pltpu.VMEM((height, width), blocks.dtype),
            pltpu.SemaphoreType.DMA((loads,)),
            pltpu.SemaphoreType.DMA((stores,)),
        ],
        compiler_params=pltpu.CompilerParams(vmem_limit_bytes=WIDE_GRANT),
        cost_estimate=pl.CostEstimate(
            flops=0,
            bytes_accessed=2 * (blocks.size + height * width),
            transcendentals=0,
        ),
        name="dense_block",
    )(row_index, col_index, tile_total, blocks)


def forward_products(matrix, shards, first, count):
    height, features = shards[0].shape
    depth = matrix.shape[2]
    parts = len(shards)

    def kernel(*refs):
        m_ref, x_refs, o_refs = refs[0], refs[1 : 1 + parts], refs[1 + parts : 1 + parts + count]
        m_buf, x_buf, o_buf, m_sem, x_sem, o_sem = refs[1 + parts + count :]

        def m_copy(block):
            rows = pl.ds(pl.multiple_of((first + block) * height, height), height)
            return pltpu.make_async_copy(m_ref.at[0, rows], m_buf.at[block], m_sem.at[block])

        def x_copy(part):
            return pltpu.make_async_copy(
                x_refs[part], x_buf.at[pl.ds(part * height, height)], x_sem.at[part]
            )

        def o_copy(block):
            return pltpu.make_async_copy(o_buf.at[block], o_refs[block], o_sem.at[block])

        m_copy(0).start()
        for part in range(parts):
            x_copy(part).start()
        for block in range(1, count):
            m_copy(block).start()
        for part in range(parts):
            x_copy(part).wait()

        @pl.loop(0, count)
        def _(block):
            m_copy(block).wait()
            o_buf[block] = jnp.dot(
                m_buf[block], x_buf[...], preferred_element_type=jnp.float32
            ).astype(o_buf.dtype)
            for index in range(count):

                @pl.when(block == index)
                def _():
                    o_copy(index).start()

        for block in range(count):
            o_copy(block).wait()

    return pl.pallas_call(
        kernel,
        out_shape=[jax.ShapeDtypeStruct((height, features), jnp.bfloat16)] * count,
        in_specs=[ANY] + [ANY] * parts,
        out_specs=[ANY] * count,
        scratch_shapes=[
            pltpu.VMEM((count, height, depth), matrix.dtype),
            pltpu.VMEM((depth, features), jnp.bfloat16),
            pltpu.VMEM((count, height, features), jnp.bfloat16),
            pltpu.SemaphoreType.DMA((count,)),
            pltpu.SemaphoreType.DMA((parts,)),
            pltpu.SemaphoreType.DMA((count,)),
        ],
        compiler_params=pltpu.CompilerParams(vmem_limit_bytes=GRANT),
        cost_estimate=pl.CostEstimate(
            flops=2 * count * height * depth * features,
            bytes_accessed=2 * (count * height * (depth + features) + depth * features),
            transcendentals=0,
        ),
        name="forward_products",
    )(matrix, *shards)


def backward_products(matrix, grads, first, count, carried, split):
    features, width = grads[0].shape
    depth = matrix.shape[1]
    parts = len(grads)
    carries = 0 if carried is None else 1
    outs = count if split else 1

    def kernel(*refs):
        m_ref, g_refs = refs[0], refs[1 : 1 + parts]
        c_refs = refs[1 + parts : 1 + parts + carries]
        o_refs = refs[1 + parts + carries : 1 + parts + carries + outs]
        rest = refs[1 + parts + carries + outs :]
        m_buf, g_buf, o_buf, m_sem, g_sem, o_sem = rest[:6]
        c_buf, c_sem = rest[6:] if carries else (None, None)

        def m_copy(block):
            columns = pl.ds(pl.multiple_of((first + block) * width, width), width)
            return pltpu.make_async_copy(m_ref.at[0, :, columns], m_buf.at[block], m_sem.at[block])

        def g_copy(part):
            return pltpu.make_async_copy(
                g_refs[part], g_buf.at[:, pl.ds(part * width, width)], g_sem.at[part]
            )

        def c_copy(block):
            return pltpu.make_async_copy(
                c_refs[0].at[:, pl.ds(pl.multiple_of(block * width, width), width)],
                c_buf.at[block],
                c_sem.at[block],
            )

        def o_copy(block):
            target = o_refs[block] if split else o_refs[0].at[:, pl.ds(block * width, width)]
            return pltpu.make_async_copy(o_buf.at[block], target, o_sem.at[block])

        m_copy(0).start()
        for part in range(parts):
            g_copy(part).start()
        for block in range(count):
            if block:
                m_copy(block).start()
            if carries:
                c_copy(block).start()
        for part in range(parts):
            g_copy(part).wait()

        @pl.loop(0, count)
        def _(block):
            m_copy(block).wait()
            total = jnp.dot(g_buf[...], m_buf[block], preferred_element_type=jnp.float32)
            if carries:
                c_copy(block).wait()
                total = total + c_buf[block].astype(jnp.float32)
            o_buf[block] = total.astype(o_buf.dtype)
            for index in range(count):

                @pl.when(block == index)
                def _():
                    o_copy(index).start()

        for block in range(count):
            o_copy(block).wait()

    shape = (features, width) if split else (features, count * width)
    scratch = [
        pltpu.VMEM((count, depth, width), matrix.dtype),
        pltpu.VMEM((features, depth), jnp.bfloat16),
        pltpu.VMEM((count, features, width), jnp.bfloat16),
        pltpu.SemaphoreType.DMA((count,)),
        pltpu.SemaphoreType.DMA((parts,)),
        pltpu.SemaphoreType.DMA((count,)),
    ]
    if carries:
        scratch += [
            pltpu.VMEM((count, features, width), jnp.bfloat16),
            pltpu.SemaphoreType.DMA((count,)),
        ]
    return pl.pallas_call(
        kernel,
        out_shape=[jax.ShapeDtypeStruct(shape, jnp.bfloat16)] * outs,
        in_specs=[ANY] + [ANY] * (parts + carries),
        out_specs=[ANY] * outs,
        scratch_shapes=scratch,
        compiler_params=pltpu.CompilerParams(vmem_limit_bytes=GRANT),
        cost_estimate=pl.CostEstimate(
            flops=2 * count * width * depth * features,
            bytes_accessed=2 * (count * width * (depth + features) + depth * features),
            transcendentals=0,
        ),
        name="backward_products",
    )(matrix, *grads, *(() if carried is None else (carried,)))


def load_all(sources, targets, sems):
    copies = [
        pltpu.make_async_copy(source, target, sems.at[index])
        for index, (source, target) in enumerate(zip(sources, targets))
    ]
    for copy in copies:
        copy.start()
    return copies


def split_pair(value, lane):
    high = value.astype(jnp.bfloat16)
    low = value - high.astype(jnp.float32)
    return jnp.where(lane == 0, high.astype(jnp.float32), low).astype(jnp.bfloat16)


def node_layer(terms, weight, bias, cotangent):
    nodes, features = cotangent.shape
    parts = len(terms)

    def kernel(*refs):
        sources = refs[: parts + 3]
        output_ref, grads_ref, terms_ref = refs[parts + 3 : parts + 6]
        t_buf, w_buf, b_buf, c_buf, sems = refs[parts + 6 :]
        targets = [t_buf.at[part] for part in range(parts)] + [w_buf, b_buf, c_buf]
        copies = load_all(sources, targets, sems)
        copies[0].wait()
        total = t_buf[0].astype(jnp.float32)
        for part in range(1, parts):
            copies[part].wait()
            total = total + t_buf[part].astype(jnp.float32)
        aggregated = total.astype(jnp.bfloat16)
        for copy in copies[parts:]:
            copy.wait()
        pre = jnp.dot(aggregated, w_buf[...], preferred_element_type=jnp.float32) + b_buf[...]
        gate = jax.nn.sigmoid(pre)
        output_ref[...] = (pre * gate).astype(jnp.bfloat16)
        grad_pre = (
            c_buf[...].astype(jnp.float32) * gate * (1.0 + pre * (1.0 - gate))
        ).astype(jnp.bfloat16)
        grads_ref[...] = lax.dot_general(
            w_buf[...],
            grad_pre,
            (((1,), (1,)), ((), ())),
            preferred_element_type=jnp.float32,
        ).astype(jnp.bfloat16)
        over_nodes = (((0,), (0,)), ((), ()))
        terms_ref[:, :features] = lax.dot_general(
            aggregated, grad_pre, over_nodes, preferred_element_type=jnp.float32
        ).astype(jnp.bfloat16)
        bias_terms = lax.dot_general(
            grad_pre,
            jnp.ones((nodes, LANES), jnp.bfloat16),
            over_nodes,
            preferred_element_type=jnp.float32,
        )
        lane = lax.broadcasted_iota(jnp.int32, bias_terms.shape, 1)
        terms_ref[:, features:] = split_pair(bias_terms, lane)

    return pl.pallas_call(
        kernel,
        out_shape=[
            jax.ShapeDtypeStruct((nodes, features), jnp.bfloat16),
            jax.ShapeDtypeStruct((features, nodes), jnp.bfloat16),
            jax.ShapeDtypeStruct((features, features + LANES), jnp.bfloat16),
        ],
        in_specs=[ANY] * (parts + 3),
        scratch_shapes=[
            pltpu.VMEM((parts, nodes, features), jnp.bfloat16),
            pltpu.VMEM((features, features), jnp.bfloat16),
            pltpu.VMEM((1, features), jnp.float32),
            pltpu.VMEM((nodes, features), jnp.bfloat16),
            pltpu.SemaphoreType.DMA((parts + 3,)),
        ],
        compiler_params=pltpu.CompilerParams(vmem_limit_bytes=GRANT),
        cost_estimate=pl.CostEstimate(
            flops=6 * nodes * features * features,
            bytes_accessed=2 * (12 * nodes * features + 2 * features * features),
            transcendentals=nodes * features,
        ),
        name="node_layer",
    )(*terms, weight, bias.reshape(1, features), cotangent)


def spread_totals(parts, features):
    chips, rows, width = parts.shape

    def kernel(parts_ref, out_ref):
        total = jnp.sum(parts_ref[...].astype(jnp.float32), axis=0)
        pair = total[:, features:]
        lane = lax.broadcasted_iota(jnp.int32, pair.shape, 1)
        bias_total = jnp.broadcast_to(pair[:, :1] + pair[:, 1:2], pair.shape)
        row = jnp.concatenate(
            [total[:, :features].astype(jnp.bfloat16), split_pair(bias_total, lane)], axis=1
        )
        out_ref[...] = jnp.broadcast_to(row[None], (chips, rows, width))

    return pl.pallas_call(
        kernel,
        out_shape=jax.ShapeDtypeStruct((chips, rows, width), jnp.bfloat16),
        compiler_params=pltpu.CompilerParams(vmem_limit_bytes=GRANT),
        cost_estimate=pl.CostEstimate(
            flops=parts.size, bytes_accessed=4 * parts.size, transcendentals=0
        ),
        name="spread_totals",
    )(parts)


def transposed_sum(terms):
    features, nodes = terms[0].shape
    parts = len(terms)

    def kernel(*refs):
        out_ref, t_buf, sems = refs[parts:]
        copies = load_all(refs[:parts], [t_buf.at[part] for part in range(parts)], sems)
        copies[0].wait()
        total = t_buf[0].astype(jnp.float32)
        for part in range(1, parts):
            copies[part].wait()
            total = total + t_buf[part].astype(jnp.float32)
        out_ref[...] = total.T.astype(jnp.bfloat16)

    return pl.pallas_call(
        kernel,
        out_shape=jax.ShapeDtypeStruct((nodes, features), jnp.bfloat16),
        in_specs=[ANY] * parts,
        scratch_shapes=[
            pltpu.VMEM((parts, features, nodes), jnp.bfloat16),
            pltpu.SemaphoreType.DMA((parts,)),
        ],
        compiler_params=pltpu.CompilerParams(vmem_limit_bytes=GRANT),
        cost_estimate=pl.CostEstimate(
            flops=parts * nodes * features,
            bytes_accessed=2 * (parts + 1) * nodes * features,
            transcendentals=0,
        ),
        name="transposed_sum",
    )(*terms)


def per_device(
    node_features, tile_values, tile_rows, tile_cols, tile_count, weight, bias, cotangent
):
    blocks = tile_values[0]
    tile = blocks.shape[-1]
    local_nodes = node_features.shape[0]
    step_tiles = local_nodes // tile
    row_tiles = step_tiles * lax.axis_size(COL_CHIPS)
    col_tiles = step_tiles * lax.axis_size(ROW_CHIPS + ("core",))
    node_total = local_nodes * lax.axis_size(ALL_CHIPS + ("core",))
    x, yh, core = lax.axis_index("x"), lax.axis_index("yh"), lax.axis_index("core")
    z, yl = lax.axis_index("z"), lax.axis_index("yl")
    steps = len(STEPS)
    features = weight.shape[0]
    chips = lax.axis_size(ALL_CHIPS)

    owner = tile_rows[0] // step_tiles
    row_place = place(owner // 2, owner % 2, z, yl) * step_tiles + tile_rows[0] % step_tiles
    owner = tile_cols[0] // step_tiles
    col_place = place(owner // 4, (owner // 2) % 2, x, yh) + steps * ((owner % 2) ^ core)
    col_place = col_place * step_tiles + tile_cols[0] % step_tiles
    matrix = dense_block(blocks, row_place, col_place, tile_count[0], row_tiles, col_tiles)

    got = {(0, 0): node_features}
    for step in ((3, 1), (1, 0)):
        got[step] = send(node_features, ROW_CHIPS, back(step))
    for step in ((1, 1), (3, 0), (0, 1)):
        got[step] = send(node_features, ROW_CHIPS, back(step))
    got[2, 1] = send(got[3, 1], ROW_CHIPS, back((3, 0)))
    got[2, 0] = send(got[1, 0], ROW_CHIPS, back((1, 0)))
    *own, matrix = lax.optimization_barrier((*(got[step] for step in STEPS), matrix))
    shards = own + [swap_cores(shard) for shard in own]

    partials = forward_products(matrix, shards, 0, FAR)
    arrived = [send(p, COL_CHIPS, s) for p, s in zip(partials, STEPS)]
    rest = forward_products(matrix, shards, FAR, steps - FAR)
    arrived += [send(p, COL_CHIPS, s) for p, s in zip(rest[:-1], STEPS[FAR:])]
    output, grads, terms = node_layer([rest[-1]] + arrived, weight, bias, cotangent)

    all_grads = [send(grads, COL_CHIPS, back(step)) for step in STEPS[:FAR]]
    parts = lax.all_to_all(
        terms.reshape(chips, features // chips, features + LANES),
        ALL_CHIPS, 0, 0, tiled=True,
    )
    all_grads += [send(grads, COL_CHIPS, back(step)) for step in STEPS[FAR:-1]]
    all_grads += [grads]
    spread = spread_totals(parts, features)
    sums = lax.all_to_all(spread, ALL_CHIPS, 0, 0, tiled=True)

    (far_out,) = backward_products(matrix, all_grads, steps, FAR, None, False)
    far_in = swap_cores(far_out)
    partials = backward_products(matrix, all_grads, 0, FAR, far_in, True)
    arrived = [send(p, ROW_CHIPS, s) for p, s in zip(partials, STEPS)]
    (near_out,) = backward_products(matrix, all_grads, steps + FAR, steps - FAR, None, False)
    near_in = swap_cores(near_out)
    rest = backward_products(matrix, all_grads, FAR, steps - FAR, near_in, True)
    arrived += [send(p, ROW_CHIPS, s) for p, s in zip(rest[:-1], STEPS[FAR:])]
    feature_grad = transposed_sum([rest[-1]] + arrived)

    sums = sums.reshape(features, features + LANES)
    other = swap_cores(sums)
    sums, other = sums.astype(jnp.float32), other.astype(jnp.float32)
    grad_scale = 1.0 / math.sqrt(node_total)
    weight_grad = (sums[:, :features] + other[:, :features]) * grad_scale
    pair, other_pair = sums[:, features : features + 2], other[:, features : features + 2]
    bias_grad = ((pair[:, 0] + pair[:, 1]) + (other_pair[:, 0] + other_pair[:, 1])) * grad_scale
    return (output, feature_grad, weight_grad, bias_grad)


def solution(mesh):
    mesh = Mesh(mesh.devices.reshape(4, 2, 2, 4, 2), ("x", "yh", "core", "z", "yl"))
    row, col = ("x", "yh", "core"), ("z", "yl")
    return jax.shard_map(
        per_device,
        mesh=mesh,
        in_specs=(
            P(col + row, None),
            P(row, col, None, None),
            P(row, col),
            P(row, col),
            P(row, col),
            P(),
            P(),
            P(row + col, None),
        ),
        out_specs=(P(row + col, None), P(col + row, None), P(), P()),
        check_vma=False,
    )
```

```python
import math

import jax
import jax.numpy as jnp
from jax import lax
from jax.experimental import pallas as pl
from jax.experimental.pallas import tpu as pltpu
from jax.sharding import Mesh, PartitionSpec as P


LANES = 128
STEPS = ((2, 1), (1, 1), (3, 1), (2, 0), (0, 1), (1, 0), (3, 0), (0, 0))
GROUPS = ((0, 2), (2, 3), (5, 3))
FAR = 5
ROW_CHIPS = ("x", "yh")
COL_CHIPS = ("z", "yl")
ALL_CHIPS = ROW_CHIPS + COL_CHIPS
GRANT = 32 * 1024 * 1024
WIDE_GRANT = 58 * 1024 * 1024
PLANES = 3
ANY = pl.BlockSpec(memory_space=pl.ANY)


def send(value, axes, step):
    far, near = step
    pairs = [
        (a * 2 + b, ((a + far) % 4) * 2 + (b ^ near)) for a in range(4) for b in range(2)
    ]
    return lax.ppermute(value, axes, pairs)


def swap_cores(value):
    return lax.ppermute(value, "core", [(0, 1), (1, 0)])


def back(step):
    return ((4 - step[0]) % 4, step[1])


def place(first, second, first_here, second_here):
    code = ((first - first_here + 4) % 4) * 2 + (second ^ second_here)
    position = jnp.zeros_like(code)
    for index, (far, near) in enumerate(STEPS):
        position = jnp.where(code == far * 2 + near, index, position)
    return position


def dense_block(blocks, row_index, col_index, tile_total, row_tiles, col_tiles):
    slots, tile, _ = blocks.shape
    height, width = row_tiles * tile, col_tiles * tile
    loads, stores, fill = 4, 8, 32
    share = slots // loads

    def kernel(rows_ref, cols_ref, total_ref, blocks_ref, out_ref, tiles, image, t_sem, s_sem):
        def load(part):
            span = pl.ds(part * share, share)
            return pltpu.make_async_copy(blocks_ref.at[span], tiles.at[span], t_sem.at[part])

        def store(part):
            span = pl.ds(part * (height // stores), height // stores)
            return pltpu.make_async_copy(image.at[span], out_ref.at[0, span], s_sem.at[part])

        for part in range(loads):
            load(part).start()

        @pl.loop(0, height // fill)
        def _(index):
            image[pl.ds(pl.multiple_of(index * fill, fill), fill)] = jnp.zeros(
                (fill, width), image.dtype
            )

        total = total_ref[0]
        for part in range(loads):
            load(part).wait()

            def put(slot, carry):
                rows = pl.ds(pl.multiple_of(rows_ref[slot] * tile, tile), tile)
                cols = pl.ds(pl.multiple_of(cols_ref[slot] * tile, tile), tile)
                image[rows, cols] = tiles[slot]
                return carry

            lax.fori_loop(part * share, jnp.minimum((part + 1) * share, total), put, 0)
        for part in range(stores):
            store(part).start()
        for part in range(stores):
            store(part).wait()

    smem = pl.BlockSpec(memory_space=pltpu.SMEM)
    return pl.pallas_call(
        kernel,
        out_shape=jax.ShapeDtypeStruct((PLANES, height, width), blocks.dtype),
        in_specs=[smem, smem, smem, ANY],
        out_specs=ANY,
        scratch_shapes=[
            pltpu.VMEM((slots, tile, tile), blocks.dtype),
            pltpu.VMEM((height, width), blocks.dtype),
            pltpu.SemaphoreType.DMA((loads,)),
            pltpu.SemaphoreType.DMA((stores,)),
        ],
        compiler_params=pltpu.CompilerParams(vmem_limit_bytes=WIDE_GRANT),
        cost_estimate=pl.CostEstimate(
            flops=0,
            bytes_accessed=2 * (blocks.size + height * width),
            transcendentals=0,
        ),
        name="dense_block",
    )(row_index, col_index, tile_total, blocks)


def forward_products(matrix, shards, first, count):
    height, features = shards[0].shape
    depth = matrix.shape[2]
    parts = len(shards)

    def kernel(*refs):
        m_ref, x_refs, o_refs = refs[0], refs[1 : 1 + parts], refs[1 + parts : 1 + parts + count]
        m_buf, x_buf, o_buf, m_sem, x_sem, o_sem = refs[1 + parts + count :]

        def m_copy(block):
            rows = pl.ds(pl.multiple_of((first + block) * height, height), height)
            return pltpu.make_async_copy(m_ref.at[0, rows], m_buf.at[block], m_sem.at[block])

        def x_copy(part):
            return pltpu.make_async_copy(
                x_refs[part], x_buf.at[pl.ds(part * height, height)], x_sem.at[part]
            )

        def o_copy(block):
            return pltpu.make_async_copy(o_buf.at[block], o_refs[block], o_sem.at[block])

        m_copy(0).start()
        for part in range(parts):
            x_copy(part).start()
        for block in range(1, count):
            m_copy(block).start()
        for part in range(parts):
            x_copy(part).wait()

        @pl.loop(0, count)
        def _(block):
            m_copy(block).wait()
            o_buf[block] = jnp.dot(
                m_buf[block], x_buf[...], preferred_element_type=jnp.float32
            ).astype(o_buf.dtype)
            for index in range(count):

                @pl.when(block == index)
                def _():
                    o_copy(index).start()

        for block in range(count):
            o_copy(block).wait()

    return pl.pallas_call(
        kernel,
        out_shape=[jax.ShapeDtypeStruct((height, features), jnp.bfloat16)] * count,
        in_specs=[ANY] + [ANY] * parts,
        out_specs=[ANY] * count,
        scratch_shapes=[
            pltpu.VMEM((count, height, depth), matrix.dtype),
            pltpu.VMEM((depth, features), jnp.bfloat16),
            pltpu.VMEM((count, height, features), jnp.bfloat16),
            pltpu.SemaphoreType.DMA((count,)),
            pltpu.SemaphoreType.DMA((parts,)),
            pltpu.SemaphoreType.DMA((count,)),
        ],
        compiler_params=pltpu.CompilerParams(vmem_limit_bytes=GRANT),
        cost_estimate=pl.CostEstimate(
            flops=2 * count * height * depth * features,
            bytes_accessed=2 * (count * height * (depth + features) + depth * features),
            transcendentals=0,
        ),
        name="forward_products",
    )(matrix, *shards)


def backward_products(matrix, grads, first, count, carried, carry_first, split):
    features, width = grads[0].shape
    depth = matrix.shape[1]
    parts = len(grads)
    carries = 0 if carried is None else 1
    outs = count if split else 1

    def kernel(*refs):
        m_ref, g_refs = refs[0], refs[1 : 1 + parts]
        c_refs = refs[1 + parts : 1 + parts + carries]
        o_refs = refs[1 + parts + carries : 1 + parts + carries + outs]
        rest = refs[1 + parts + carries + outs :]
        m_buf, g_buf, o_buf, m_sem, g_sem, o_sem = rest[:6]
        c_buf, c_sem = rest[6:] if carries else (None, None)

        def m_copy(block):
            columns = pl.ds(pl.multiple_of((first + block) * width, width), width)
            return pltpu.make_async_copy(m_ref.at[0, :, columns], m_buf.at[block], m_sem.at[block])

        def g_copy(part):
            return pltpu.make_async_copy(
                g_refs[part], g_buf.at[:, pl.ds(part * width, width)], g_sem.at[part]
            )

        def c_copy(block):
            return pltpu.make_async_copy(
                c_refs[0].at[:, pl.ds(pl.multiple_of((carry_first + block) * width, width), width)],
                c_buf.at[block],
                c_sem.at[block],
            )

        def o_copy(block):
            target = o_refs[block] if split else o_refs[0].at[:, pl.ds(block * width, width)]
            return pltpu.make_async_copy(o_buf.at[block], target, o_sem.at[block])

        m_copy(0).start()
        for part in range(parts):
            g_copy(part).start()
        for block in range(count):
            if block:
                m_copy(block).start()
            if carries:
                c_copy(block).start()
        for part in range(parts):
            g_copy(part).wait()

        @pl.loop(0, count)
        def _(block):
            m_copy(block).wait()
            total = jnp.dot(g_buf[...], m_buf[block], preferred_element_type=jnp.float32)
            if carries:
                c_copy(block).wait()
                total = total + c_buf[block].astype(jnp.float32)
            o_buf[block] = total.astype(o_buf.dtype)
            for index in range(count):

                @pl.when(block == index)
                def _():
                    o_copy(index).start()

        for block in range(count):
            o_copy(block).wait()

    shape = (features, width) if split else (features, count * width)
    scratch = [
        pltpu.VMEM((count, depth, width), matrix.dtype),
        pltpu.VMEM((features, depth), jnp.bfloat16),
        pltpu.VMEM((count, features, width), jnp.bfloat16),
        pltpu.SemaphoreType.DMA((count,)),
        pltpu.SemaphoreType.DMA((parts,)),
        pltpu.SemaphoreType.DMA((count,)),
    ]
    if carries:
        scratch += [
            pltpu.VMEM((count, features, width), jnp.bfloat16),
            pltpu.SemaphoreType.DMA((count,)),
        ]
    return pl.pallas_call(
        kernel,
        out_shape=[jax.ShapeDtypeStruct(shape, jnp.bfloat16)] * outs,
        in_specs=[ANY] + [ANY] * (parts + carries),
        out_specs=[ANY] * outs,
        scratch_shapes=scratch,
        compiler_params=pltpu.CompilerParams(vmem_limit_bytes=GRANT),
        cost_estimate=pl.CostEstimate(
            flops=2 * count * width * depth * features,
            bytes_accessed=2 * (count * width * (depth + features) + depth * features),
            transcendentals=0,
        ),
        name="backward_products",
    )(matrix, *grads, *(() if carried is None else (carried,)))


def load_all(sources, targets, sems):
    copies = [
        pltpu.make_async_copy(source, target, sems.at[index])
        for index, (source, target) in enumerate(zip(sources, targets))
    ]
    for copy in copies:
        copy.start()
    return copies


def split_pair(value, lane):
    high = value.astype(jnp.bfloat16)
    low = value - high.astype(jnp.float32)
    return jnp.where(lane == 0, high.astype(jnp.float32), low).astype(jnp.bfloat16)


def node_layer(terms, weight, bias, cotangent):
    nodes, features = cotangent.shape
    parts = len(terms)

    def kernel(*refs):
        sources = refs[: parts + 3]
        output_ref, grads_ref, terms_ref = refs[parts + 3 : parts + 6]
        t_buf, w_buf, b_buf, c_buf, sems = refs[parts + 6 :]
        targets = [t_buf.at[part] for part in range(parts)] + [w_buf, b_buf, c_buf]
        copies = load_all(sources, targets, sems)
        copies[0].wait()
        total = t_buf[0].astype(jnp.float32)
        for part in range(1, parts):
            copies[part].wait()
            total = total + t_buf[part].astype(jnp.float32)
        aggregated = total.astype(jnp.bfloat16)
        for copy in copies[parts:]:
            copy.wait()
        pre = jnp.dot(aggregated, w_buf[...], preferred_element_type=jnp.float32) + b_buf[...]
        gate = jax.nn.sigmoid(pre)
        output_ref[...] = (pre * gate).astype(jnp.bfloat16)
        grad_pre = (
            c_buf[...].astype(jnp.float32) * gate * (1.0 + pre * (1.0 - gate))
        ).astype(jnp.bfloat16)
        grads_ref[...] = lax.dot_general(
            w_buf[...],
            grad_pre,
            (((1,), (1,)), ((), ())),
            preferred_element_type=jnp.float32,
        ).astype(jnp.bfloat16)
        over_nodes = (((0,), (0,)), ((), ()))
        terms_ref[:, :features] = lax.dot_general(
            aggregated, grad_pre, over_nodes, preferred_element_type=jnp.float32
        ).astype(jnp.bfloat16)
        bias_terms = lax.dot_general(
            grad_pre,
            jnp.ones((nodes, LANES), jnp.bfloat16),
            over_nodes,
            preferred_element_type=jnp.float32,
        )
        lane = lax.broadcasted_iota(jnp.int32, bias_terms.shape, 1)
        terms_ref[:, features:] = split_pair(bias_terms, lane)

    return pl.pallas_call(
        kernel,
        out_shape=[
            jax.ShapeDtypeStruct((nodes, features), jnp.bfloat16),
            jax.ShapeDtypeStruct((features, nodes), jnp.bfloat16),
            jax.ShapeDtypeStruct((features, features + LANES), jnp.bfloat16),
        ],
        in_specs=[ANY] * (parts + 3),
        scratch_shapes=[
            pltpu.VMEM((parts, nodes, features), jnp.bfloat16),
            pltpu.VMEM((features, features), jnp.bfloat16),
            pltpu.VMEM((1, features), jnp.float32),
            pltpu.VMEM((nodes, features), jnp.bfloat16),
            pltpu.SemaphoreType.DMA((parts + 3,)),
        ],
        compiler_params=pltpu.CompilerParams(vmem_limit_bytes=GRANT),
        cost_estimate=pl.CostEstimate(
            flops=6 * nodes * features * features,
            bytes_accessed=2 * (12 * nodes * features + 2 * features * features),
            transcendentals=nodes * features,
        ),
        name="node_layer",
    )(*terms, weight, bias.reshape(1, features), cotangent)


def spread_totals(parts, features):
    chips, rows, width = parts.shape

    def kernel(parts_ref, out_ref):
        total = jnp.sum(parts_ref[...].astype(jnp.float32), axis=0)
        pair = total[:, features:]
        lane = lax.broadcasted_iota(jnp.int32, pair.shape, 1)
        bias_total = jnp.broadcast_to(pair[:, :1] + pair[:, 1:2], pair.shape)
        row = jnp.concatenate(
            [total[:, :features].astype(jnp.bfloat16), split_pair(bias_total, lane)], axis=1
        )
        out_ref[...] = jnp.broadcast_to(row[None], (chips, rows, width))

    return pl.pallas_call(
        kernel,
        out_shape=jax.ShapeDtypeStruct((chips, rows, width), jnp.bfloat16),
        compiler_params=pltpu.CompilerParams(vmem_limit_bytes=GRANT),
        cost_estimate=pl.CostEstimate(
            flops=parts.size, bytes_accessed=4 * parts.size, transcendentals=0
        ),
        name="spread_totals",
    )(parts)


def transposed_sum(terms):
    features, nodes = terms[0].shape
    parts = len(terms)

    def kernel(*refs):
        out_ref, t_buf, sems = refs[parts:]
        copies = load_all(refs[:parts], [t_buf.at[part] for part in range(parts)], sems)
        copies[0].wait()
        total = t_buf[0].astype(jnp.float32)
        for part in range(1, parts):
            copies[part].wait()
            total = total + t_buf[part].astype(jnp.float32)
        out_ref[...] = total.T.astype(jnp.bfloat16)

    return pl.pallas_call(
        kernel,
        out_shape=jax.ShapeDtypeStruct((nodes, features), jnp.bfloat16),
        in_specs=[ANY] * parts,
        scratch_shapes=[
            pltpu.VMEM((parts, features, nodes), jnp.bfloat16),
            pltpu.SemaphoreType.DMA((parts,)),
        ],
        compiler_params=pltpu.CompilerParams(vmem_limit_bytes=GRANT),
        cost_estimate=pl.CostEstimate(
            flops=parts * nodes * features,
            bytes_accessed=2 * (parts + 1) * nodes * features,
            transcendentals=0,
        ),
        name="transposed_sum",
    )(*terms)


def per_device(
    node_features, tile_values, tile_rows, tile_cols, tile_count, weight, bias, cotangent
):
    blocks = tile_values[0]
    tile = blocks.shape[-1]
    local_nodes = node_features.shape[0]
    step_tiles = local_nodes // tile
    row_tiles = step_tiles * lax.axis_size(COL_CHIPS)
    col_tiles = step_tiles * lax.axis_size(ROW_CHIPS + ("core",))
    node_total = local_nodes * lax.axis_size(ALL_CHIPS + ("core",))
    x, yh, core = lax.axis_index("x"), lax.axis_index("yh"), lax.axis_index("core")
    z, yl = lax.axis_index("z"), lax.axis_index("yl")
    steps = len(STEPS)
    features = weight.shape[0]
    chips = lax.axis_size(ALL_CHIPS)

    owner = tile_rows[0] // step_tiles
    row_place = place(owner // 2, owner % 2, z, yl) * step_tiles + tile_rows[0] % step_tiles
    owner = tile_cols[0] // step_tiles
    col_place = place(owner // 4, (owner // 2) % 2, x, yh) + steps * ((owner % 2) ^ core)
    col_place = col_place * step_tiles + tile_cols[0] % step_tiles
    matrix = dense_block(blocks, row_place, col_place, tile_count[0], row_tiles, col_tiles)

    got = {(0, 0): node_features}
    for step in ((3, 1), (1, 0)):
        got[step] = send(node_features, ROW_CHIPS, back(step))
    for step in ((1, 1), (3, 0), (0, 1)):
        got[step] = send(node_features, ROW_CHIPS, back(step))
    got[2, 1] = send(got[3, 1], ROW_CHIPS, back((3, 0)))
    got[2, 0] = send(got[1, 0], ROW_CHIPS, back((1, 0)))
    late = ((1, 1), (3, 0), (0, 1), (2, 1), (2, 0))
    swapped = {step: swap_cores(got[step]) for step in got if step not in late}
    *held, matrix = lax.optimization_barrier((*(got[step] for step in late), matrix))
    got.update(zip(late, held))
    swapped.update({step: swap_cores(got[step]) for step in late})
    shards = [got[step] for step in STEPS] + [swapped[step] for step in STEPS]

    arrived = []
    for first, count in GROUPS:
        partials = forward_products(matrix, shards, first, count)
        for partial, step in zip(partials, STEPS[first : first + count]):
            arrived.append(partial if step == (0, 0) else send(partial, COL_CHIPS, step))
    output, grads, terms = node_layer(arrived[::-1], weight, bias, cotangent)

    all_grads = [send(grads, COL_CHIPS, back(step)) for step in STEPS[:4]]
    parts = lax.all_to_all(
        terms.reshape(chips, features // chips, features + LANES),
        ALL_CHIPS, 0, 0, tiled=True,
    )
    all_grads += [send(grads, COL_CHIPS, back(step)) for step in STEPS[4:-1]]
    all_grads += [grads]
    spread = spread_totals(parts, features)
    sums = lax.all_to_all(spread, ALL_CHIPS, 0, 0, tiled=True)

    (far,) = backward_products(matrix, all_grads, steps, FAR, None, 0, False)
    far = swap_cores(far)
    (near,) = backward_products(matrix, all_grads, steps + FAR, steps - FAR, None, 0, False)
    near = swap_cores(near)
    arrived = []
    for first, count in GROUPS:
        carried, carry_first = (far, first) if first < FAR else (near, first - FAR)
        partials = backward_products(matrix, all_grads, first, count, carried, carry_first, True)
        for partial, step in zip(partials, STEPS[first : first + count]):
            arrived.append(partial if step == (0, 0) else send(partial, ROW_CHIPS, step))
    feature_grad = transposed_sum(arrived[::-1])

    sums = sums.reshape(features, features + LANES)
    other = swap_cores(sums)
    sums, other = sums.astype(jnp.float32), other.astype(jnp.float32)
    grad_scale = 1.0 / math.sqrt(node_total)
    weight_grad = (sums[:, :features] + other[:, :features]) * grad_scale
    pair, other_pair = sums[:, features : features + 2], other[:, features : features + 2]
    bias_grad = ((pair[:, 0] + pair[:, 1]) + (other_pair[:, 0] + other_pair[:, 1])) * grad_scale
    return (output, feature_grad, weight_grad, bias_grad)


def solution(mesh):
    mesh = Mesh(mesh.devices.reshape(4, 2, 2, 4, 2), ("x", "yh", "core", "z", "yl"))
    row, col = ("x", "yh", "core"), ("z", "yl")
    return jax.shard_map(
        per_device,
        mesh=mesh,
        in_specs=(
            P(col + row, None),
            P(row, col, None, None),
            P(row, col),
            P(row, col),
            P(row, col),
            P(),
            P(),
            P(row + col, None),
        ),
        out_specs=(P(row + col, None), P(col + row, None), P(), P()),
        check_vma=False,
    )
```

```python
import math

import jax
import jax.numpy as jnp
from jax import lax
from jax.experimental import pallas as pl
from jax.experimental.pallas import tpu as pltpu
from jax.sharding import Mesh, PartitionSpec as P


LANES = 128
STEPS = ((2, 1), (1, 1), (3, 1), (2, 0), (0, 0), (0, 1), (1, 0), (3, 0))
GROUPS = ((0, 4), (4, 4))
EARLY = 5
ROW_CHIPS = ("x", "yh")
COL_CHIPS = ("z", "yl")
ALL_CHIPS = ROW_CHIPS + COL_CHIPS
GRANT = 32 * 1024 * 1024
WIDE_GRANT = 58 * 1024 * 1024
PLANES = 3
EARLY_PLANES = 5
ANY = pl.BlockSpec(memory_space=pl.ANY)


def send(value, axes, step):
    far, near = step
    pairs = [
        (a * 2 + b, ((a + far) % 4) * 2 + (b ^ near)) for a in range(4) for b in range(2)
    ]
    return lax.ppermute(value, axes, pairs)


def swap_cores(value):
    return lax.ppermute(value, "core", [(0, 1), (1, 0)])


def own_first(terms):
    own = STEPS.index((0, 0))
    return [terms[own]] + terms[:own] + terms[own + 1 :]


def back(step):
    return ((4 - step[0]) % 4, step[1])


def place(first, second, first_here, second_here):
    code = ((first - first_here + 4) % 4) * 2 + (second ^ second_here)
    position = jnp.zeros_like(code)
    for index, (far, near) in enumerate(STEPS):
        position = jnp.where(code == far * 2 + near, index, position)
    return position


def dense_block(blocks, row_index, col_index, tile_total, row_tiles, col_tiles):
    slots, tile, _ = blocks.shape
    height, width = row_tiles * tile, col_tiles * tile
    loads, stores, fill = 4, 8, 32
    share = slots // loads

    def kernel(rows_ref, cols_ref, total_ref, blocks_ref, out_ref, tiles, image, t_sem, s_sem):
        def load(part):
            span = pl.ds(part * share, share)
            return pltpu.make_async_copy(blocks_ref.at[span], tiles.at[span], t_sem.at[part])

        def store(part):
            span = pl.ds(part * (height // stores), height // stores)
            return pltpu.make_async_copy(image.at[span], out_ref.at[0, span], s_sem.at[part])

        for part in range(loads):
            load(part).start()

        @pl.loop(0, height // fill)
        def _(index):
            image[pl.ds(pl.multiple_of(index * fill, fill), fill)] = jnp.zeros(
                (fill, width), image.dtype
            )

        total = total_ref[0]
        for part in range(loads):
            load(part).wait()

            def put(slot, carry):
                rows = pl.ds(pl.multiple_of(rows_ref[slot] * tile, tile), tile)
                cols = pl.ds(pl.multiple_of(cols_ref[slot] * tile, tile), tile)
                image[rows, cols] = tiles[slot]
                return carry

            lax.fori_loop(part * share, jnp.minimum((part + 1) * share, total), put, 0)
        for part in range(stores):
            store(part).start()
        for part in range(stores):
            store(part).wait()

    smem = pl.BlockSpec(memory_space=pltpu.SMEM)
    return pl.pallas_call(
        kernel,
        out_shape=jax.ShapeDtypeStruct((PLANES, height, width), blocks.dtype),
        in_specs=[smem, smem, smem, ANY],
        out_specs=ANY,
        scratch_shapes=[
            pltpu.VMEM((slots, tile, tile), blocks.dtype),
            pltpu.VMEM((height, width), blocks.dtype),
            pltpu.SemaphoreType.DMA((loads,)),
            pltpu.SemaphoreType.DMA((stores,)),
        ],
        compiler_params=pltpu.CompilerParams(vmem_limit_bytes=WIDE_GRANT),
        cost_estimate=pl.CostEstimate(
            flops=0,
            bytes_accessed=2 * (blocks.size + height * width),
            transcendentals=0,
        ),
        name="dense_block",
    )(row_index, col_index, tile_total, blocks)


def forward_products(matrix, shards, first, count):
    height, features = shards[0].shape
    depth = matrix.shape[2]
    parts = len(shards)

    def kernel(*refs):
        m_ref, x_refs, o_refs = refs[0], refs[1 : 1 + parts], refs[1 + parts : 1 + parts + count]
        m_buf, x_buf, o_buf, m_sem, x_sem, o_sem = refs[1 + parts + count :]

        def m_copy(block):
            rows = pl.ds(pl.multiple_of((first + block) * height, height), height)
            return pltpu.make_async_copy(m_ref.at[0, rows], m_buf.at[block], m_sem.at[block])

        def x_copy(part):
            return pltpu.make_async_copy(
                x_refs[part], x_buf.at[pl.ds(part * height, height)], x_sem.at[part]
            )

        def o_copy(block):
            return pltpu.make_async_copy(o_buf.at[block], o_refs[block], o_sem.at[block])

        m_copy(0).start()
        for part in range(parts):
            x_copy(part).start()
        for block in range(1, count):
            m_copy(block).start()
        for part in range(parts):
            x_copy(part).wait()

        @pl.loop(0, count)
        def _(block):
            m_copy(block).wait()
            o_buf[block] = jnp.dot(
                m_buf[block], x_buf[...], preferred_element_type=jnp.float32
            ).astype(o_buf.dtype)
            for index in range(count):

                @pl.when(block == index)
                def _():
                    o_copy(index).start()

        for block in range(count):
            o_copy(block).wait()

    return pl.pallas_call(
        kernel,
        out_shape=[jax.ShapeDtypeStruct((height, features), jnp.bfloat16)] * count,
        in_specs=[ANY] + [ANY] * parts,
        out_specs=[ANY] * count,
        scratch_shapes=[
            pltpu.VMEM((count, height, depth), matrix.dtype),
            pltpu.VMEM((depth, features), jnp.bfloat16),
            pltpu.VMEM((count, height, features), jnp.bfloat16),
            pltpu.SemaphoreType.DMA((count,)),
            pltpu.SemaphoreType.DMA((parts,)),
            pltpu.SemaphoreType.DMA((count,)),
        ],
        compiler_params=pltpu.CompilerParams(vmem_limit_bytes=GRANT),
        cost_estimate=pl.CostEstimate(
            flops=2 * count * height * depth * features,
            bytes_accessed=2 * (count * height * (depth + features) + depth * features),
            transcendentals=0,
        ),
        name="forward_products",
    )(matrix, *shards)


def backward_products(matrix, grads, place, first, count, carried, kind, split, planes=0):
    features, width = grads[0].shape
    parts = len(grads)
    depth = parts * width
    carries = len(carried)
    outs = count if split else 1

    def kernel(*refs):
        m_ref, g_refs = refs[0], refs[1 : 1 + parts]
        c_refs = refs[1 + parts : 1 + parts + carries]
        o_refs = refs[1 + parts + carries : 1 + parts + carries + outs]
        rest = refs[1 + parts + carries + outs :]
        m_buf, g_buf, o_buf, m_sem, g_sem, o_sem = rest[:6]
        c_bufs, c_sems = rest[6 : 6 + carries], rest[6 + carries :]

        def m_copy(block):
            columns = pl.ds(pl.multiple_of((first + block) * width, width), width)
            rows = pl.ds(place * width, depth)
            return pltpu.make_async_copy(
                m_ref.at[0, rows, columns], m_buf.at[block], m_sem.at[block]
            )

        def g_copy(part):
            return pltpu.make_async_copy(
                g_refs[part], g_buf.at[:, pl.ds(part * width, width)], g_sem.at[part]
            )

        def c_copy(carry, block):
            start = (carried[carry][1] + block) * width
            source = c_refs[carry].at[0] if len(carried[carry][0].shape) == 3 else c_refs[carry]
            return pltpu.make_async_copy(
                source.at[:, pl.ds(pl.multiple_of(start, width), width)],
                c_bufs[carry].at[block],
                c_sems[carry].at[block],
            )

        def o_copy(block):
            columns = pl.ds(block * width, width)
            if split:
                target = o_refs[block]
            else:
                target = o_refs[0].at[0, :, columns] if planes else o_refs[0].at[:, columns]
            return pltpu.make_async_copy(o_buf.at[block], target, o_sem.at[block])

        m_copy(0).start()
        for part in range(parts):
            g_copy(part).start()
        for block in range(count):
            if block:
                m_copy(block).start()
            for carry in range(carries):
                c_copy(carry, block).start()
        for part in range(parts):
            g_copy(part).wait()

        @pl.loop(0, count)
        def _(block):
            m_copy(block).wait()
            total = jnp.dot(g_buf[...], m_buf[block], preferred_element_type=jnp.float32)
            for carry in range(carries):
                c_copy(carry, block).wait()
                total = total + c_bufs[carry][block].astype(jnp.float32)
            o_buf[block] = total.astype(o_buf.dtype)
            for index in range(count):

                @pl.when(block == index)
                def _():
                    o_copy(index).start()

        for block in range(count):
            o_copy(block).wait()

    shape = (features, width) if split else (features, count * width)
    shape = (planes,) + shape if planes else shape
    return pl.pallas_call(
        kernel,
        out_shape=[jax.ShapeDtypeStruct(shape, kind)] * outs,
        in_specs=[ANY] * (1 + parts + carries),
        out_specs=[ANY] * outs,
        scratch_shapes=[
            pltpu.VMEM((count, depth, width), matrix.dtype),
            pltpu.VMEM((features, depth), jnp.bfloat16),
            pltpu.VMEM((count, features, width), kind),
            pltpu.SemaphoreType.DMA((count,)),
            pltpu.SemaphoreType.DMA((parts,)),
            pltpu.SemaphoreType.DMA((count,)),
        ]
        + [pltpu.VMEM((count, features, width), array.dtype) for array, _ in carried]
        + [pltpu.SemaphoreType.DMA((count,)) for _ in carried],
        compiler_params=pltpu.CompilerParams(vmem_limit_bytes=GRANT),
        cost_estimate=pl.CostEstimate(
            flops=2 * count * width * depth * features,
            bytes_accessed=2 * (count * width * (depth + features) + depth * features),
            transcendentals=0,
        ),
        name="backward_products",
    )(matrix, *grads, *(array for array, _ in carried))


def load_all(sources, targets, sems):
    copies = [
        pltpu.make_async_copy(source, target, sems.at[index])
        for index, (source, target) in enumerate(zip(sources, targets))
    ]
    for copy in copies:
        copy.start()
    return copies


def split_pair(value, lane):
    high = value.astype(jnp.bfloat16)
    low = value - high.astype(jnp.float32)
    return jnp.where(lane == 0, high.astype(jnp.float32), low).astype(jnp.bfloat16)


def node_layer(terms, weight, bias, cotangent):
    nodes, features = cotangent.shape
    parts = len(terms)

    def kernel(*refs):
        sources = refs[: parts + 3]
        output_ref, grads_ref, terms_ref = refs[parts + 3 : parts + 6]
        t_buf, w_buf, b_buf, c_buf, sems = refs[parts + 6 :]
        targets = [t_buf.at[part] for part in range(parts)] + [w_buf, b_buf, c_buf]
        copies = load_all(sources, targets, sems)
        copies[0].wait()
        total = t_buf[0].astype(jnp.float32)
        for part in range(1, parts):
            copies[part].wait()
            total = total + t_buf[part].astype(jnp.float32)
        aggregated = total.astype(jnp.bfloat16)
        for copy in copies[parts:]:
            copy.wait()
        pre = jnp.dot(aggregated, w_buf[...], preferred_element_type=jnp.float32) + b_buf[...]
        gate = jax.nn.sigmoid(pre)
        output_ref[...] = (pre * gate).astype(jnp.bfloat16)
        grad_pre = (
            c_buf[...].astype(jnp.float32) * gate * (1.0 + pre * (1.0 - gate))
        ).astype(jnp.bfloat16)
        grads_ref[...] = lax.dot_general(
            w_buf[...],
            grad_pre,
            (((1,), (1,)), ((), ())),
            preferred_element_type=jnp.float32,
        ).astype(jnp.bfloat16)
        over_nodes = (((0,), (0,)), ((), ()))
        terms_ref[:, :features] = lax.dot_general(
            aggregated, grad_pre, over_nodes, preferred_element_type=jnp.float32
        ).astype(jnp.bfloat16)
        bias_terms = lax.dot_general(
            grad_pre,
            jnp.ones((nodes, LANES), jnp.bfloat16),
            over_nodes,
            preferred_element_type=jnp.float32,
        )
        lane = lax.broadcasted_iota(jnp.int32, bias_terms.shape, 1)
        terms_ref[:, features:] = split_pair(bias_terms, lane)

    return pl.pallas_call(
        kernel,
        out_shape=[
            jax.ShapeDtypeStruct((nodes, features), jnp.bfloat16),
            jax.ShapeDtypeStruct((features, nodes), jnp.bfloat16),
            jax.ShapeDtypeStruct((features, features + LANES), jnp.bfloat16),
        ],
        in_specs=[ANY] * (parts + 3),
        scratch_shapes=[
            pltpu.VMEM((parts, nodes, features), jnp.bfloat16),
            pltpu.VMEM((features, features), jnp.bfloat16),
            pltpu.VMEM((1, features), jnp.float32),
            pltpu.VMEM((nodes, features), jnp.bfloat16),
            pltpu.SemaphoreType.DMA((parts + 3,)),
        ],
        compiler_params=pltpu.CompilerParams(vmem_limit_bytes=GRANT),
        cost_estimate=pl.CostEstimate(
            flops=6 * nodes * features * features,
            bytes_accessed=2 * (12 * nodes * features + 2 * features * features),
            transcendentals=nodes * features,
        ),
        name="node_layer",
    )(*terms, weight, bias.reshape(1, features), cotangent)


def spread_totals(parts, features):
    chips, rows, width = parts.shape

    def kernel(parts_ref, out_ref):
        total = jnp.sum(parts_ref[...].astype(jnp.float32), axis=0)
        pair = total[:, features:]
        lane = lax.broadcasted_iota(jnp.int32, pair.shape, 1)
        bias_total = jnp.broadcast_to(pair[:, :1] + pair[:, 1:2], pair.shape)
        row = jnp.concatenate(
            [total[:, :features].astype(jnp.bfloat16), split_pair(bias_total, lane)], axis=1
        )
        out_ref[...] = jnp.broadcast_to(row[None], (chips, rows, width))

    return pl.pallas_call(
        kernel,
        out_shape=jax.ShapeDtypeStruct((chips, rows, width), jnp.bfloat16),
        compiler_params=pltpu.CompilerParams(vmem_limit_bytes=GRANT),
        cost_estimate=pl.CostEstimate(
            flops=parts.size, bytes_accessed=4 * parts.size, transcendentals=0
        ),
        name="spread_totals",
    )(parts)


def block_sum(terms, finish):
    features, nodes = terms[0].shape
    parts = len(terms)

    def kernel(*refs):
        out_ref, bufs, sems = refs[parts], refs[parts + 1 : -1], refs[-1]
        copies = load_all(refs[:parts], bufs, sems)
        copies[0].wait()
        total = bufs[0][...].astype(jnp.float32)
        for part in range(1, parts):
            copies[part].wait()
            total = total + bufs[part][...].astype(jnp.float32)
        out_ref[...] = total.T.astype(jnp.bfloat16) if finish else total

    shape = (nodes, features) if finish else (features, nodes)
    return pl.pallas_call(
        kernel,
        out_shape=jax.ShapeDtypeStruct(shape, jnp.bfloat16 if finish else jnp.float32),
        in_specs=[ANY] * parts,
        scratch_shapes=[pltpu.VMEM((features, nodes), term.dtype) for term in terms]
        + [pltpu.SemaphoreType.DMA((parts,))],
        compiler_params=pltpu.CompilerParams(vmem_limit_bytes=GRANT),
        cost_estimate=pl.CostEstimate(
            flops=parts * nodes * features,
            bytes_accessed=2 * (parts + 1) * nodes * features,
            transcendentals=0,
        ),
        name="block_sum",
    )(*terms)


def per_device(
    node_features, tile_values, tile_rows, tile_cols, tile_count, weight, bias, cotangent
):
    blocks = tile_values[0]
    tile = blocks.shape[-1]
    local_nodes = node_features.shape[0]
    step_tiles = local_nodes // tile
    row_tiles = step_tiles * lax.axis_size(COL_CHIPS)
    col_tiles = step_tiles * lax.axis_size(ROW_CHIPS + ("core",))
    node_total = local_nodes * lax.axis_size(ALL_CHIPS + ("core",))
    x, yh, core = lax.axis_index("x"), lax.axis_index("yh"), lax.axis_index("core")
    z, yl = lax.axis_index("z"), lax.axis_index("yl")
    steps = len(STEPS)
    features = weight.shape[0]
    chips = lax.axis_size(ALL_CHIPS)

    owner = tile_rows[0] // step_tiles
    row_place = place(owner // 2, owner % 2, z, yl) * step_tiles + tile_rows[0] % step_tiles
    owner = tile_cols[0] // step_tiles
    col_place = place(owner // 4, (owner // 2) % 2, x, yh) + steps * ((owner % 2) ^ core)
    col_place = col_place * step_tiles + tile_cols[0] % step_tiles
    matrix = dense_block(blocks, row_place, col_place, tile_count[0], row_tiles, col_tiles)

    got = {(0, 0): node_features}
    for step in ((3, 1), (1, 0)):
        got[step] = send(node_features, ROW_CHIPS, back(step))
    for step in ((1, 1), (3, 0), (0, 1)):
        got[step] = send(node_features, ROW_CHIPS, back(step))
    got[2, 1] = send(got[3, 1], ROW_CHIPS, back((3, 0)))
    got[2, 0] = send(got[1, 0], ROW_CHIPS, back((1, 0)))
    late = ((1, 1), (3, 0), (0, 1), (2, 1), (2, 0))
    swapped = {step: swap_cores(got[step]) for step in got if step not in late}
    *held, matrix = lax.optimization_barrier((*(got[step] for step in late), matrix))
    got.update(zip(late, held))
    swapped.update({step: swap_cores(got[step]) for step in late})
    shards = [got[step] for step in STEPS] + [swapped[step] for step in STEPS]

    arrived = []
    for first, count in GROUPS:
        partials = forward_products(matrix, shards, first, count)
        for partial, step in zip(partials, STEPS[first : first + count]):
            arrived.append(partial if step == (0, 0) else send(partial, COL_CHIPS, step))
    output, grads, terms = node_layer(own_first(arrived), weight, bias, cotangent)

    early = [send(grads, COL_CHIPS, back(step)) for step in STEPS[: EARLY - 1]] + [grads]
    parts = lax.all_to_all(
        terms.reshape(chips, features // chips, features + LANES),
        ALL_CHIPS, 0, 0, tiled=True,
    )
    late = [send(grads, COL_CHIPS, back(step)) for step in STEPS[EARLY:]]

    (part,) = backward_products(
        matrix, early, 0, 0, 2 * steps, (), jnp.float32, False, EARLY_PLANES
    )

    def late_products(first, count, carried, split):
        return backward_products(
            matrix, late, EARLY, first, count, carried, jnp.bfloat16, split
        )

    spread = spread_totals(parts, features)
    sums = lax.all_to_all(spread, ALL_CHIPS, 0, 0, tiled=True)
    swapped = []
    for first, count in GROUPS:
        (other,) = late_products(
            steps + first, count, ((part, steps + first),), False
        )
        swapped.append(swap_cores(other))
    arrived = []
    for index, (first, count) in enumerate(GROUPS):
        partials = late_products(
            first, count, ((part, first), (swapped[index], 0)), True
        )
        for partial, step in zip(partials, STEPS[first : first + count]):
            arrived.append(partial if step == (0, 0) else send(partial, ROW_CHIPS, step))

    sums = sums.reshape(features, features + LANES)
    other = swap_cores(sums)
    sums, other = sums.astype(jnp.float32), other.astype(jnp.float32)
    grad_scale = 1.0 / math.sqrt(node_total)
    weight_grad = (sums[:, :features] + other[:, :features]) * grad_scale
    pair, other_pair = sums[:, features : features + 2], other[:, features : features + 2]
    bias_grad = ((pair[:, 0] + pair[:, 1]) + (other_pair[:, 0] + other_pair[:, 1])) * grad_scale

    own = STEPS.index((0, 0))
    total = block_sum([arrived[own]] + arrived[: EARLY - 1], False)
    weight_grad, bias_grad, total = lax.optimization_barrier((weight_grad, bias_grad, total))
    feature_grad = block_sum([total] + arrived[EARLY:], True)
    return (output, feature_grad, weight_grad, bias_grad)


def solution(mesh):
    mesh = Mesh(mesh.devices.reshape(4, 2, 2, 4, 2), ("x", "yh", "core", "z", "yl"))
    row, col = ("x", "yh", "core"), ("z", "yl")
    return jax.shard_map(
        per_device,
        mesh=mesh,
        in_specs=(
            P(col + row, None),
            P(row, col, None, None),
            P(row, col),
            P(row, col),
            P(row, col),
            P(),
            P(),
            P(row + col, None),
        ),
        out_specs=(P(row + col, None), P(col + row, None), P(), P()),
        check_vma=False,
    )
```

```python
import math

import jax
import jax.numpy as jnp
from jax import lax
from jax.experimental import pallas as pl
from jax.experimental.pallas import tpu as pltpu
from jax.sharding import Mesh, PartitionSpec as P


LANES = 128
STEPS = ((2, 1), (1, 1), (3, 1), (2, 0), (0, 0), (0, 1), (1, 0), (3, 0))
GROUPS = ((0, 4), (4, 4))
FIRST_STEPS = ((3, 1), (1, 0))
SEND_STEPS = ((1, 1), (3, 0), (0, 1))
LATE_STEPS = SEND_STEPS + ((2, 1), (2, 0))
ROW_CHIPS = ("x", "yh")
COL_CHIPS = ("z", "yl")
ALL_CHIPS = ROW_CHIPS + COL_CHIPS
GRANT = 32 * 1024 * 1024
WIDE_GRANT = 58 * 1024 * 1024
PLANES = 5
ANY = pl.BlockSpec(memory_space=pl.ANY)


def send(value, axes, step):
    far, near = step
    pairs = [
        (a * 2 + b, ((a + far) % 4) * 2 + (b ^ near)) for a in range(4) for b in range(2)
    ]
    return lax.ppermute(value, axes, pairs)


def swap_cores(value):
    return lax.ppermute(value, "core", [(0, 1), (1, 0)])


def own_first(terms):
    own = STEPS.index((0, 0))
    return [terms[own]] + terms[:own] + terms[own + 1 :]


def back(step):
    return ((4 - step[0]) % 4, step[1])


def place(first, second, first_here, second_here):
    code = ((first - first_here + 4) % 4) * 2 + (second ^ second_here)
    position = jnp.zeros_like(code)
    for index, (far, near) in enumerate(STEPS):
        position = jnp.where(code == far * 2 + near, index, position)
    return position


def dense_block(blocks, row_index, col_index, tile_total, row_tiles, col_tiles):
    slots, tile, _ = blocks.shape
    height, width = row_tiles * tile, col_tiles * tile
    loads, stores, fill = 4, 4, 32
    share = slots // loads
    half = width // 2

    def kernel(
        rows_ref, cols_ref, total_ref, blocks_ref, own_ref, other_ref, tiles, image, t_sem, s_sem
    ):
        def load(part):
            span = pl.ds(part * share, share)
            return pltpu.make_async_copy(blocks_ref.at[span], tiles.at[span], t_sem.at[part])

        def store(part):
            span = pl.ds(part // 2 * (height // stores), height // stores)
            target = other_ref.at[span] if part % 2 else own_ref.at[0, span]
            return pltpu.make_async_copy(
                image.at[span, pl.ds(part % 2 * half, half)], target, s_sem.at[part]
            )

        for part in range(loads):
            load(part).start()

        @pl.loop(0, height // fill)
        def _(index):
            image[pl.ds(pl.multiple_of(index * fill, fill), fill)] = jnp.zeros(
                (fill, width), image.dtype
            )

        total = total_ref[0]
        for part in range(loads):
            load(part).wait()

            def put(slot, carry):
                rows = pl.ds(pl.multiple_of(rows_ref[slot] * tile, tile), tile)
                cols = pl.ds(pl.multiple_of(cols_ref[slot] * tile, tile), tile)
                image[rows, cols] = tiles[slot]
                return carry

            lax.fori_loop(part * share, jnp.minimum((part + 1) * share, total), put, 0)
        for part in range(2 * stores):
            store(part).start()
        for part in range(2 * stores):
            store(part).wait()

    smem = pl.BlockSpec(memory_space=pltpu.SMEM)
    return pl.pallas_call(
        kernel,
        out_shape=[
            jax.ShapeDtypeStruct((PLANES, height, half), blocks.dtype),
            jax.ShapeDtypeStruct((height, half), blocks.dtype),
        ],
        in_specs=[smem, smem, smem, ANY],
        out_specs=[ANY, ANY],
        scratch_shapes=[
            pltpu.VMEM((slots, tile, tile), blocks.dtype),
            pltpu.VMEM((height, width), blocks.dtype),
            pltpu.SemaphoreType.DMA((loads,)),
            pltpu.SemaphoreType.DMA((2 * stores,)),
        ],
        compiler_params=pltpu.CompilerParams(vmem_limit_bytes=WIDE_GRANT),
        cost_estimate=pl.CostEstimate(
            flops=0,
            bytes_accessed=2 * (blocks.size + height * width),
            transcendentals=0,
        ),
        name="dense_block",
    )(row_index, col_index, tile_total, blocks)


def products(own, other, panels, first, count, backward):
    parts = len(panels)
    size = panels[0].shape[1 if backward else 0]
    features = panels[0].shape[0 if backward else 1]
    depth = parts * size
    half = depth // 2

    def kernel(*refs):
        own_ref, other_ref, p_refs = refs[0], refs[1], refs[2 : 2 + parts]
        o_refs = refs[2 + parts : 2 + parts + count]
        m_buf, p_buf, o_buf, m_sem, p_sem, o_sem = refs[2 + parts + count :]

        def m_copy(block, side):
            span = pl.ds(pl.multiple_of((first + block) * size, size), size)
            source = other_ref if side else own_ref.at[0]
            if backward:
                source, target = source.at[:, span], m_buf.at[block, pl.ds(side * half, half)]
            else:
                source, target = source.at[span], m_buf.at[block, :, pl.ds(side * half, half)]
            return pltpu.make_async_copy(source, target, m_sem.at[block, side])

        def p_copy(part):
            span = pl.ds(part * size, size)
            target = p_buf.at[:, span] if backward else p_buf.at[span]
            return pltpu.make_async_copy(p_refs[part], target, p_sem.at[part])

        def o_copy(block):
            return pltpu.make_async_copy(o_buf.at[block], o_refs[block], o_sem.at[block])

        for part in range(parts):
            p_copy(part).start()
        for block in range(count):
            for side in range(2):
                m_copy(block, side).start()
        for part in range(parts):
            p_copy(part).wait()

        @pl.loop(0, count)
        def _(block):
            for side in range(2):
                m_copy(block, side).wait()
            left, right = (p_buf[...], m_buf[block]) if backward else (m_buf[block], p_buf[...])
            o_buf[block] = jnp.dot(left, right, preferred_element_type=jnp.float32).astype(
                o_buf.dtype
            )
            for index in range(count):

                @pl.when(block == index)
                def _():
                    o_copy(index).start()

        for block in range(count):
            o_copy(block).wait()

    shape = panels[0].shape
    return pl.pallas_call(
        kernel,
        out_shape=[jax.ShapeDtypeStruct(shape, jnp.bfloat16)] * count,
        in_specs=[ANY] * (2 + parts),
        out_specs=[ANY] * count,
        scratch_shapes=[
            pltpu.VMEM((count, depth, size) if backward else (count, size, depth), own.dtype),
            pltpu.VMEM((features, depth) if backward else (depth, features), jnp.bfloat16),
            pltpu.VMEM((count,) + shape, jnp.bfloat16),
            pltpu.SemaphoreType.DMA((count, 2)),
            pltpu.SemaphoreType.DMA((parts,)),
            pltpu.SemaphoreType.DMA((count,)),
        ],
        compiler_params=pltpu.CompilerParams(vmem_limit_bytes=GRANT),
        cost_estimate=pl.CostEstimate(
            flops=2 * count * size * depth * features,
            bytes_accessed=2 * (count * size * (depth + features) + depth * features),
            transcendentals=0,
        ),
        name="backward_products" if backward else "forward_products",
    )(own, other, *panels)


def load_all(sources, targets, sems):
    copies = [
        pltpu.make_async_copy(source, target, sems.at[index])
        for index, (source, target) in enumerate(zip(sources, targets))
    ]
    for copy in copies:
        copy.start()
    return copies


def split_pair(value, lane):
    high = value.astype(jnp.bfloat16)
    low = value - high.astype(jnp.float32)
    return jnp.where(lane == 0, high.astype(jnp.float32), low).astype(jnp.bfloat16)


def node_layer(terms, weight, bias, cotangent):
    nodes, features = cotangent.shape
    parts = len(terms)

    def kernel(*refs):
        sources = refs[: parts + 3]
        output_ref, grads_ref, terms_ref = refs[parts + 3 : parts + 6]
        t_buf, w_buf, b_buf, c_buf, sems = refs[parts + 6 :]
        targets = [t_buf.at[part] for part in range(parts)] + [w_buf, b_buf, c_buf]
        copies = load_all(sources, targets, sems)
        copies[0].wait()
        total = t_buf[0].astype(jnp.float32)
        for part in range(1, parts):
            copies[part].wait()
            total = total + t_buf[part].astype(jnp.float32)
        aggregated = total.astype(jnp.bfloat16)
        for copy in copies[parts:]:
            copy.wait()
        pre = jnp.dot(aggregated, w_buf[...], preferred_element_type=jnp.float32) + b_buf[...]
        gate = jax.nn.sigmoid(pre)
        output_ref[...] = (pre * gate).astype(jnp.bfloat16)
        grad_pre = (
            c_buf[...].astype(jnp.float32) * gate * (1.0 + pre * (1.0 - gate))
        ).astype(jnp.bfloat16)
        grads_ref[...] = lax.dot_general(
            w_buf[...],
            grad_pre,
            (((1,), (1,)), ((), ())),
            preferred_element_type=jnp.float32,
        ).astype(jnp.bfloat16)
        over_nodes = (((0,), (0,)), ((), ()))
        terms_ref[:, :features] = lax.dot_general(
            aggregated, grad_pre, over_nodes, preferred_element_type=jnp.float32
        ).astype(jnp.bfloat16)
        bias_terms = lax.dot_general(
            grad_pre,
            jnp.ones((nodes, LANES), jnp.bfloat16),
            over_nodes,
            preferred_element_type=jnp.float32,
        )
        lane = lax.broadcasted_iota(jnp.int32, bias_terms.shape, 1)
        terms_ref[:, features:] = split_pair(bias_terms, lane)

    return pl.pallas_call(
        kernel,
        out_shape=[
            jax.ShapeDtypeStruct((nodes, features), jnp.bfloat16),
            jax.ShapeDtypeStruct((features, nodes), jnp.bfloat16),
            jax.ShapeDtypeStruct((features, features + LANES), jnp.bfloat16),
        ],
        in_specs=[ANY] * (parts + 3),
        scratch_shapes=[
            pltpu.VMEM((parts, nodes, features), jnp.bfloat16),
            pltpu.VMEM((features, features), jnp.bfloat16),
            pltpu.VMEM((1, features), jnp.float32),
            pltpu.VMEM((nodes, features), jnp.bfloat16),
            pltpu.SemaphoreType.DMA((parts + 3,)),
        ],
        compiler_params=pltpu.CompilerParams(vmem_limit_bytes=GRANT),
        cost_estimate=pl.CostEstimate(
            flops=6 * nodes * features * features,
            bytes_accessed=2 * (12 * nodes * features + 2 * features * features),
            transcendentals=nodes * features,
        ),
        name="node_layer",
    )(*terms, weight, bias.reshape(1, features), cotangent)


def spread_totals(parts, features):
    chips, rows, width = parts.shape

    def kernel(parts_ref, out_ref):
        total = jnp.sum(parts_ref[...].astype(jnp.float32), axis=0)
        pair = total[:, features:]
        lane = lax.broadcasted_iota(jnp.int32, pair.shape, 1)
        bias_total = jnp.broadcast_to(pair[:, :1] + pair[:, 1:2], pair.shape)
        row = jnp.concatenate(
            [total[:, :features].astype(jnp.bfloat16), split_pair(bias_total, lane)], axis=1
        )
        out_ref[...] = jnp.broadcast_to(row[None], (chips, rows, width))

    return pl.pallas_call(
        kernel,
        out_shape=jax.ShapeDtypeStruct((chips, rows, width), jnp.bfloat16),
        compiler_params=pltpu.CompilerParams(vmem_limit_bytes=GRANT),
        cost_estimate=pl.CostEstimate(
            flops=parts.size, bytes_accessed=4 * parts.size, transcendentals=0
        ),
        name="spread_totals",
    )(parts)


def block_sum(terms, finish):
    features, nodes = terms[0].shape
    parts = len(terms)

    def kernel(*refs):
        out_ref, bufs, sems = refs[parts], refs[parts + 1 : -1], refs[-1]
        copies = load_all(refs[:parts], bufs, sems)
        copies[0].wait()
        total = bufs[0][...].astype(jnp.float32)
        for part in range(1, parts):
            copies[part].wait()
            total = total + bufs[part][...].astype(jnp.float32)
        out_ref[...] = total.T.astype(jnp.bfloat16) if finish else total

    shape = (nodes, features) if finish else (features, nodes)
    return pl.pallas_call(
        kernel,
        out_shape=jax.ShapeDtypeStruct(shape, jnp.bfloat16 if finish else jnp.float32),
        in_specs=[ANY] * parts,
        scratch_shapes=[pltpu.VMEM((features, nodes), term.dtype) for term in terms]
        + [pltpu.SemaphoreType.DMA((parts,))],
        compiler_params=pltpu.CompilerParams(vmem_limit_bytes=GRANT),
        cost_estimate=pl.CostEstimate(
            flops=parts * nodes * features,
            bytes_accessed=2 * (parts + 1) * nodes * features,
            transcendentals=0,
        ),
        name="block_sum",
    )(*terms)


def per_device(
    node_features, tile_values, tile_rows, tile_cols, tile_count, weight, bias, cotangent
):
    blocks = tile_values[0]
    tile = blocks.shape[-1]
    local_nodes = node_features.shape[0]
    step_tiles = local_nodes // tile
    row_tiles = step_tiles * lax.axis_size(COL_CHIPS)
    col_tiles = step_tiles * lax.axis_size(ROW_CHIPS + ("core",))
    node_total = local_nodes * lax.axis_size(ALL_CHIPS + ("core",))
    x, yh, core = lax.axis_index("x"), lax.axis_index("yh"), lax.axis_index("core")
    z, yl = lax.axis_index("z"), lax.axis_index("yl")
    steps = len(STEPS)
    features = weight.shape[0]
    chips = lax.axis_size(ALL_CHIPS)

    owner = tile_rows[0] // step_tiles
    row_place = place(owner // 2, owner % 2, z, yl) * step_tiles + tile_rows[0] % step_tiles
    owner = tile_cols[0] // step_tiles
    col_place = place(owner // 4, (owner // 2) % 2, x, yh) + steps * ((owner % 2) ^ core)
    col_place = col_place * step_tiles + tile_cols[0] % step_tiles
    own_half, other_half = dense_block(blocks, row_place, col_place, tile_count[0], row_tiles, col_tiles)

    got = {(0, 0): node_features}
    for step in FIRST_STEPS:
        got[step] = send(node_features, ROW_CHIPS, back(step))
    for step in SEND_STEPS:
        got[step] = send(node_features, ROW_CHIPS, back(step))
    got[2, 1] = send(got[3, 1], ROW_CHIPS, back((3, 0)))
    got[2, 0] = send(got[1, 0], ROW_CHIPS, back((1, 0)))
    swapped = {step: swap_cores(got[step]) for step in got if step not in LATE_STEPS}
    *held, own_half, other_half = lax.optimization_barrier(
        (*(got[step] for step in LATE_STEPS), own_half, other_half)
    )
    got.update(zip(LATE_STEPS, held))
    swapped.update({step: swap_cores(got[step]) for step in LATE_STEPS})
    panels = [got[step] for step in STEPS] + [swapped[step] for step in STEPS]
    their_half = swap_cores(other_half)

    arrived = []
    for first, count in GROUPS:
        partials = products(own_half, other_half, panels, first, count, False)
        for partial, step in zip(partials, STEPS[first : first + count]):
            arrived.append(partial if step == (0, 0) else send(partial, COL_CHIPS, step))
    output, grads, terms = node_layer(own_first(arrived), weight, bias, cotangent)

    got = {(0, 0): grads}
    for step in FIRST_STEPS:
        got[step] = send(grads, COL_CHIPS, back(step))
    for step in SEND_STEPS:
        got[step] = send(grads, COL_CHIPS, back(step))
    parts = lax.all_to_all(
        terms.reshape(chips, features // chips, features + LANES),
        ALL_CHIPS, 0, 0, tiled=True,
    )
    got[2, 1] = send(got[3, 1], COL_CHIPS, back((3, 0)))
    got[2, 0] = send(got[1, 0], COL_CHIPS, back((1, 0)))
    swapped = {step: swap_cores(got[step]) for step in got}
    spread = spread_totals(parts, features)
    sums = lax.all_to_all(spread, ALL_CHIPS, 0, 0, tiled=True)

    panels = [got[step] for step in STEPS] + [swapped[step] for step in STEPS]
    arrived = []
    for first, count in GROUPS:
        partials = products(own_half, their_half, panels, first, count, True)
        for partial, step in zip(partials, STEPS[first : first + count]):
            arrived.append(partial if step == (0, 0) else send(partial, ROW_CHIPS, step))

    sums = sums.reshape(features, features + LANES)
    other = swap_cores(sums)
    sums, other = sums.astype(jnp.float32), other.astype(jnp.float32)
    grad_scale = 1.0 / math.sqrt(node_total)
    weight_grad = (sums[:, :features] + other[:, :features]) * grad_scale
    pair, other_pair = sums[:, features : features + 2], other[:, features : features + 2]
    bias_grad = ((pair[:, 0] + pair[:, 1]) + (other_pair[:, 0] + other_pair[:, 1])) * grad_scale

    own = STEPS.index((0, 0))
    total = block_sum([arrived[own]] + arrived[:own], False)
    weight_grad, bias_grad, total = lax.optimization_barrier((weight_grad, bias_grad, total))
    feature_grad = block_sum([total] + arrived[own + 1 :], True)
    return (output, feature_grad, weight_grad, bias_grad)


def solution(mesh):
    mesh = Mesh(mesh.devices.reshape(4, 2, 2, 4, 2), ("x", "yh", "core", "z", "yl"))
    row, col = ("x", "yh", "core"), ("z", "yl")
    return jax.shard_map(
        per_device,
        mesh=mesh,
        in_specs=(
            P(col + row, None),
            P(row, col, None, None),
            P(row, col),
            P(row, col),
            P(row, col),
            P(),
            P(),
            P(row + col, None),
        ),
        out_specs=(P(row + col, None), P(col + row, None), P(), P()),
        check_vma=False,
    )
```

```python
import math

import jax
import jax.numpy as jnp
from jax import lax
from jax.experimental import pallas as pl
from jax.experimental.pallas import tpu as pltpu
from jax.sharding import Mesh, PartitionSpec as P


LANES = 128
STEPS = ((2, 1), (1, 1), (3, 1), (2, 0), (0, 0), (0, 1), (1, 0), (3, 0))
GROUPS = ((0, 4), (4, 4))
FIRST_STEPS = ((3, 1), (1, 0))
SEND_STEPS = ((1, 1), (3, 0), (0, 1))
LATE_STEPS = SEND_STEPS + ((2, 1), (2, 0))
ROW_CHIPS = ("x", "yh")
COL_CHIPS = ("z", "yl")
ALL_CHIPS = ROW_CHIPS + COL_CHIPS
GRANT = 32 * 1024 * 1024
WIDE_GRANT = 58 * 1024 * 1024
PLANES = 5
PANEL_PLANES = 9
ANY = pl.BlockSpec(memory_space=pl.ANY)


def send(value, axes, step):
    far, near = step
    pairs = [
        (a * 2 + b, ((a + far) % 4) * 2 + (b ^ near)) for a in range(4) for b in range(2)
    ]
    return lax.ppermute(value, axes, pairs)


def swap_cores(value):
    return lax.ppermute(value, "core", [(0, 1), (1, 0)])


def own_first(terms):
    own = STEPS.index((0, 0))
    return [terms[own]] + terms[:own] + terms[own + 1 :]


def back(step):
    return ((4 - step[0]) % 4, step[1])


def place(first, second, first_here, second_here):
    code = ((first - first_here + 4) % 4) * 2 + (second ^ second_here)
    position = jnp.zeros_like(code)
    for index, (far, near) in enumerate(STEPS):
        position = jnp.where(code == far * 2 + near, index, position)
    return position


def dense_block(blocks, row_index, col_index, tile_total, row_tiles, col_tiles):
    slots, tile, _ = blocks.shape
    height, width = row_tiles * tile, col_tiles * tile
    loads, stores, fill = 4, 4, 32
    share = slots // loads
    half = width // 2

    def kernel(
        rows_ref, cols_ref, total_ref, blocks_ref, own_ref, other_ref, tiles, image, t_sem, s_sem
    ):
        def load(part):
            span = pl.ds(part * share, share)
            return pltpu.make_async_copy(blocks_ref.at[span], tiles.at[span], t_sem.at[part])

        def store(part):
            span = pl.ds(part // 2 * (height // stores), height // stores)
            target = other_ref.at[span] if part % 2 else own_ref.at[0, span]
            return pltpu.make_async_copy(
                image.at[span, pl.ds(part % 2 * half, half)], target, s_sem.at[part]
            )

        for part in range(loads):
            load(part).start()
        total = total_ref[0]
        for upper in range(2):

            @pl.loop(0, height // fill // 2)
            def _(index):
                start = upper * (height // 2) + index * fill
                image[pl.ds(pl.multiple_of(start, fill), fill)] = jnp.zeros(
                    (fill, width), image.dtype
                )

            def put(slot, carry):
                row = rows_ref[slot]

                @pl.when(row // (row_tiles // 2) == upper)
                def _():
                    rows = pl.ds(pl.multiple_of(row * tile, tile), tile)
                    cols = pl.ds(pl.multiple_of(cols_ref[slot] * tile, tile), tile)
                    image[rows, cols] = tiles[slot]

                return carry

            for part in range(loads):
                if not upper:
                    load(part).wait()
                lax.fori_loop(part * share, jnp.minimum((part + 1) * share, total), put, 0)
            for part in range(upper * stores, (upper + 1) * stores):
                store(part).start()
        for part in range(2 * stores):
            store(part).wait()

    smem = pl.BlockSpec(memory_space=pltpu.SMEM)
    return pl.pallas_call(
        kernel,
        out_shape=[
            jax.ShapeDtypeStruct((PLANES, height, half), blocks.dtype),
            jax.ShapeDtypeStruct((height, half), blocks.dtype),
        ],
        in_specs=[smem, smem, smem, ANY],
        out_specs=[ANY, ANY],
        scratch_shapes=[
            pltpu.VMEM((slots, tile, tile), blocks.dtype),
            pltpu.VMEM((height, width), blocks.dtype),
            pltpu.SemaphoreType.DMA((loads,)),
            pltpu.SemaphoreType.DMA((2 * stores,)),
        ],
        compiler_params=pltpu.CompilerParams(vmem_limit_bytes=WIDE_GRANT),
        cost_estimate=pl.CostEstimate(
            flops=0,
            bytes_accessed=2 * (blocks.size + height * width),
            transcendentals=0,
        ),
        name="dense_block",
    )(row_index, col_index, tile_total, blocks)


def products(own, other, panels, first, count, backward, keep):
    joined = not isinstance(panels, list)
    if joined:
        panels = [panels]
        features, depth = panels[0].shape[1:] if backward else panels[0].shape[:0:-1]
        size = depth // (2 * len(STEPS))
    else:
        size = panels[0].shape[1 if backward else 0]
        features = panels[0].shape[0 if backward else 1]
        depth = len(panels) * size
    parts = len(panels)
    half = depth // 2
    outs = count + (1 if keep else 0)

    def kernel(*refs):
        own_ref, other_ref, p_refs = refs[0], refs[1], refs[2 : 2 + parts]
        o_refs = refs[2 + parts : 2 + parts + outs]
        m_buf, p_buf, o_buf, m_sem, p_sem, o_sem, k_sem = refs[2 + parts + outs :]

        def m_copy(block, side):
            span = pl.ds(pl.multiple_of((first + block) * size, size), size)
            source = other_ref if side else own_ref.at[0]
            if backward:
                source, target = source.at[:, span], m_buf.at[block, pl.ds(side * half, half)]
            else:
                source, target = source.at[span], m_buf.at[block, :, pl.ds(side * half, half)]
            return pltpu.make_async_copy(source, target, m_sem.at[block, side])

        def p_copy(part):
            if joined:
                return pltpu.make_async_copy(p_refs[0].at[0], p_buf, p_sem.at[0])
            span = pl.ds(part * size, size)
            target = p_buf.at[:, span] if backward else p_buf.at[span]
            return pltpu.make_async_copy(p_refs[part], target, p_sem.at[part])

        def o_copy(block):
            return pltpu.make_async_copy(o_buf.at[block], o_refs[block], o_sem.at[block])

        for part in range(parts):
            p_copy(part).start()
        for side in range(2):
            m_copy(0, side).start()
        for part in range(parts):
            p_copy(part).wait()
        for block in range(1, count):
            for side in range(2):
                m_copy(block, side).start()
        if keep:
            kept = pltpu.make_async_copy(p_buf, o_refs[count].at[0], k_sem)
            kept.start()

        @pl.loop(0, count)
        def _(block):
            for side in range(2):
                m_copy(block, side).wait()
            left, right = (p_buf[...], m_buf[block]) if backward else (m_buf[block], p_buf[...])
            o_buf[block] = jnp.dot(left, right, preferred_element_type=jnp.float32).astype(
                o_buf.dtype
            )
            for index in range(count):

                @pl.when(block == index)
                def _():
                    o_copy(index).start()

        for block in range(count):
            o_copy(block).wait()
        if keep:
            kept.wait()

    shape = (features, size) if backward else (size, features)
    panel = (features, depth) if backward else (depth, features)
    out_shape = [jax.ShapeDtypeStruct(shape, jnp.bfloat16)] * count
    if keep:
        out_shape = out_shape + [jax.ShapeDtypeStruct((PANEL_PLANES,) + panel, jnp.bfloat16)]
    return pl.pallas_call(
        kernel,
        out_shape=out_shape,
        in_specs=[ANY] * (2 + parts),
        out_specs=[ANY] * outs,
        scratch_shapes=[
            pltpu.VMEM((count, depth, size) if backward else (count, size, depth), own.dtype),
            pltpu.VMEM(panel, jnp.bfloat16),
            pltpu.VMEM((count,) + shape, jnp.bfloat16),
            pltpu.SemaphoreType.DMA((count, 2)),
            pltpu.SemaphoreType.DMA((parts,)),
            pltpu.SemaphoreType.DMA((count,)),
            pltpu.SemaphoreType.DMA,
        ],
        compiler_params=pltpu.CompilerParams(vmem_limit_bytes=GRANT),
        cost_estimate=pl.CostEstimate(
            flops=2 * count * size * depth * features,
            bytes_accessed=2 * (count * size * (depth + features) + depth * features),
            transcendentals=0,
        ),
        name="backward_products" if backward else "forward_products",
    )(own, other, *panels)


def load_all(sources, targets, sems):
    copies = [
        pltpu.make_async_copy(source, target, sems.at[index])
        for index, (source, target) in enumerate(zip(sources, targets))
    ]
    for copy in copies:
        copy.start()
    return copies


def split_pair(value, lane):
    high = value.astype(jnp.bfloat16)
    low = value - high.astype(jnp.float32)
    return jnp.where(lane == 0, high.astype(jnp.float32), low).astype(jnp.bfloat16)


def node_layer(terms, weight, bias, cotangent):
    nodes, features = cotangent.shape
    parts = len(terms)

    def kernel(*refs):
        sources = refs[: parts + 3]
        output_ref, grads_ref, terms_ref = refs[parts + 3 : parts + 6]
        t_buf, w_buf, b_buf, c_buf, sems = refs[parts + 6 :]
        targets = [t_buf.at[part] for part in range(parts)] + [w_buf, b_buf, c_buf]
        copies = load_all(sources, targets, sems)
        copies[0].wait()
        total = t_buf[0].astype(jnp.float32)
        for part in range(1, parts):
            copies[part].wait()
            total = total + t_buf[part].astype(jnp.float32)
        aggregated = total.astype(jnp.bfloat16)
        for copy in copies[parts:]:
            copy.wait()
        pre = jnp.dot(aggregated, w_buf[...], preferred_element_type=jnp.float32) + b_buf[...]
        gate = jax.nn.sigmoid(pre)
        output_ref[...] = (pre * gate).astype(jnp.bfloat16)
        grad_pre = (
            c_buf[...].astype(jnp.float32) * gate * (1.0 + pre * (1.0 - gate))
        ).astype(jnp.bfloat16)
        grads_ref[...] = lax.dot_general(
            w_buf[...],
            grad_pre,
            (((1,), (1,)), ((), ())),
            preferred_element_type=jnp.float32,
        ).astype(jnp.bfloat16)
        over_nodes = (((0,), (0,)), ((), ()))
        terms_ref[:, :features] = lax.dot_general(
            aggregated, grad_pre, over_nodes, preferred_element_type=jnp.float32
        ).astype(jnp.bfloat16)
        bias_terms = lax.dot_general(
            grad_pre,
            jnp.ones((nodes, LANES), jnp.bfloat16),
            over_nodes,
            preferred_element_type=jnp.float32,
        )
        lane = lax.broadcasted_iota(jnp.int32, bias_terms.shape, 1)
        terms_ref[:, features:] = split_pair(bias_terms, lane)

    return pl.pallas_call(
        kernel,
        out_shape=[
            jax.ShapeDtypeStruct((nodes, features), jnp.bfloat16),
            jax.ShapeDtypeStruct((features, nodes), jnp.bfloat16),
            jax.ShapeDtypeStruct((features, features + LANES), jnp.bfloat16),
        ],
        in_specs=[ANY] * (parts + 3),
        scratch_shapes=[
            pltpu.VMEM((parts, nodes, features), jnp.bfloat16),
            pltpu.VMEM((features, features), jnp.bfloat16),
            pltpu.VMEM((1, features), jnp.float32),
            pltpu.VMEM((nodes, features), jnp.bfloat16),
            pltpu.SemaphoreType.DMA((parts + 3,)),
        ],
        compiler_params=pltpu.CompilerParams(vmem_limit_bytes=GRANT),
        cost_estimate=pl.CostEstimate(
            flops=6 * nodes * features * features,
            bytes_accessed=2 * (12 * nodes * features + 2 * features * features),
            transcendentals=nodes * features,
        ),
        name="node_layer",
    )(*terms, weight, bias.reshape(1, features), cotangent)


def spread_totals(parts, features):
    chips, rows, width = parts.shape

    def kernel(parts_ref, out_ref):
        total = jnp.sum(parts_ref[...].astype(jnp.float32), axis=0)
        pair = total[:, features:]
        lane = lax.broadcasted_iota(jnp.int32, pair.shape, 1)
        bias_total = jnp.broadcast_to(pair[:, :1] + pair[:, 1:2], pair.shape)
        row = jnp.concatenate(
            [total[:, :features].astype(jnp.bfloat16), split_pair(bias_total, lane)], axis=1
        )
        out_ref[...] = jnp.broadcast_to(row[None], (chips, rows, width))

    return pl.pallas_call(
        kernel,
        out_shape=jax.ShapeDtypeStruct((chips, rows, width), jnp.bfloat16),
        compiler_params=pltpu.CompilerParams(vmem_limit_bytes=GRANT),
        cost_estimate=pl.CostEstimate(
            flops=parts.size, bytes_accessed=4 * parts.size, transcendentals=0
        ),
        name="spread_totals",
    )(parts)


def block_sum(terms, finish):
    features, nodes = terms[0].shape
    parts = len(terms)

    def kernel(*refs):
        out_ref, bufs, sems = refs[parts], refs[parts + 1 : -1], refs[-1]
        copies = load_all(refs[:parts], bufs, sems)
        copies[0].wait()
        total = bufs[0][...].astype(jnp.float32)
        for part in range(1, parts):
            copies[part].wait()
            total = total + bufs[part][...].astype(jnp.float32)
        out_ref[...] = total.T.astype(jnp.bfloat16) if finish else total

    shape = (nodes, features) if finish else (features, nodes)
    return pl.pallas_call(
        kernel,
        out_shape=jax.ShapeDtypeStruct(shape, jnp.bfloat16 if finish else jnp.float32),
        in_specs=[ANY] * parts,
        scratch_shapes=[pltpu.VMEM((features, nodes), term.dtype) for term in terms]
        + [pltpu.SemaphoreType.DMA((parts,))],
        compiler_params=pltpu.CompilerParams(vmem_limit_bytes=GRANT),
        cost_estimate=pl.CostEstimate(
            flops=parts * nodes * features,
            bytes_accessed=2 * (parts + 1) * nodes * features,
            transcendentals=0,
        ),
        name="block_sum",
    )(*terms)


def per_device(
    node_features, tile_values, tile_rows, tile_cols, tile_count, weight, bias, cotangent
):
    blocks = tile_values[0]
    tile = blocks.shape[-1]
    local_nodes = node_features.shape[0]
    step_tiles = local_nodes // tile
    row_tiles = step_tiles * lax.axis_size(COL_CHIPS)
    col_tiles = step_tiles * lax.axis_size(ROW_CHIPS + ("core",))
    node_total = local_nodes * lax.axis_size(ALL_CHIPS + ("core",))
    x, yh, core = lax.axis_index("x"), lax.axis_index("yh"), lax.axis_index("core")
    z, yl = lax.axis_index("z"), lax.axis_index("yl")
    steps = len(STEPS)
    features = weight.shape[0]
    chips = lax.axis_size(ALL_CHIPS)

    owner = tile_rows[0] // step_tiles
    row_place = place(owner // 2, owner % 2, z, yl) * step_tiles + tile_rows[0] % step_tiles
    owner = tile_cols[0] // step_tiles
    col_place = place(owner // 4, (owner // 2) % 2, x, yh) + steps * ((owner % 2) ^ core)
    col_place = col_place * step_tiles + tile_cols[0] % step_tiles
    own_half, other_half = dense_block(blocks, row_place, col_place, tile_count[0], row_tiles, col_tiles)

    got = {(0, 0): node_features}
    for step in FIRST_STEPS:
        got[step] = send(node_features, ROW_CHIPS, back(step))
    for step in SEND_STEPS:
        got[step] = send(node_features, ROW_CHIPS, back(step))
    got[2, 1] = send(got[3, 1], ROW_CHIPS, back((3, 0)))
    got[2, 0] = send(got[1, 0], ROW_CHIPS, back((1, 0)))
    swapped = {step: swap_cores(got[step]) for step in got if step not in LATE_STEPS}
    *held, own_half, other_half = lax.optimization_barrier(
        (*(got[step] for step in LATE_STEPS), own_half, other_half)
    )
    got.update(zip(LATE_STEPS, held))
    swapped.update({step: swap_cores(got[step]) for step in LATE_STEPS})
    panels = [got[step] for step in STEPS] + [swapped[step] for step in STEPS]
    their_half = swap_cores(other_half)

    arrived = []
    for first, count in GROUPS:
        partials = products(own_half, other_half, panels, first, count, False, False)
        for partial, step in zip(partials, STEPS[first : first + count]):
            arrived.append(partial if step == (0, 0) else send(partial, COL_CHIPS, step))
    output, grads, terms = node_layer(own_first(arrived), weight, bias, cotangent)

    got = {(0, 0): grads}
    for step in FIRST_STEPS:
        got[step] = send(grads, COL_CHIPS, back(step))
    for step in SEND_STEPS:
        got[step] = send(grads, COL_CHIPS, back(step))
    parts = lax.all_to_all(
        terms.reshape(chips, features // chips, features + LANES),
        ALL_CHIPS, 0, 0, tiled=True,
    )
    got[2, 1] = send(got[3, 1], COL_CHIPS, back((3, 0)))
    got[2, 0] = send(got[1, 0], COL_CHIPS, back((1, 0)))
    swapped = {step: swap_cores(got[step]) for step in got if step not in LATE_STEPS}
    swapped.update({step: swap_cores(got[step]) for step in LATE_STEPS})
    spread = spread_totals(parts, features)
    sums = lax.all_to_all(spread, ALL_CHIPS, 0, 0, tiled=True)

    panels = [got[step] for step in STEPS] + [swapped[step] for step in STEPS]
    arrived = []
    for index, (first, count) in enumerate(GROUPS):
        partials = products(own_half, their_half, panels, first, count, True, index == 0)
        if index == 0:
            *partials, panels = partials
        for partial, step in zip(partials, STEPS[first : first + count]):
            arrived.append(partial if step == (0, 0) else send(partial, ROW_CHIPS, step))

    sums = sums.reshape(features, features + LANES)
    other = swap_cores(sums)
    sums, other = sums.astype(jnp.float32), other.astype(jnp.float32)
    grad_scale = 1.0 / math.sqrt(node_total)
    weight_grad = (sums[:, :features] + other[:, :features]) * grad_scale
    pair, other_pair = sums[:, features : features + 2], other[:, features : features + 2]
    bias_grad = ((pair[:, 0] + pair[:, 1]) + (other_pair[:, 0] + other_pair[:, 1])) * grad_scale

    own = STEPS.index((0, 0))
    total = block_sum([arrived[own]] + arrived[:own], False)
    weight_grad, bias_grad, total = lax.optimization_barrier((weight_grad, bias_grad, total))
    feature_grad = block_sum([total] + arrived[own + 1 :], True)
    return (output, feature_grad, weight_grad, bias_grad)


def solution(mesh):
    mesh = Mesh(mesh.devices.reshape(4, 2, 2, 4, 2), ("x", "yh", "core", "z", "yl"))
    row, col = ("x", "yh", "core"), ("z", "yl")
    return jax.shard_map(
        per_device,
        mesh=mesh,
        in_specs=(
            P(col + row, None),
            P(row, col, None, None),
            P(row, col),
            P(row, col),
            P(row, col),
            P(),
            P(),
            P(row + col, None),
        ),
        out_specs=(P(row + col, None), P(col + row, None), P(), P()),
        check_vma=False,
    )
```

```python
import math

import jax
import jax.numpy as jnp
from jax import lax
from jax.experimental import pallas as pl
from jax.experimental.pallas import tpu as pltpu
from jax.sharding import Mesh, PartitionSpec as P


LANES = 128
STEPS = ((2, 1), (1, 1), (3, 1), (2, 0), (0, 0), (0, 1), (1, 0), (3, 0))
GROUPS = ((0, 4), (4, 4))
FIRST_STEPS = ((3, 1), (1, 0))
SEND_STEPS = ((1, 1), (3, 0), (0, 1))
LATE_STEPS = SEND_STEPS + ((2, 1), (2, 0))
ROW_CHIPS = ("x", "yh")
COL_CHIPS = ("z", "yl")
ALL_CHIPS = ROW_CHIPS + COL_CHIPS
GRANT = 32 * 1024 * 1024
WIDE_GRANT = 58 * 1024 * 1024
PLANES = 5
PANEL_PLANES = 9
ANY = pl.BlockSpec(memory_space=pl.ANY)


def send(value, axes, step):
    far, near = step
    pairs = [
        (a * 2 + b, ((a + far) % 4) * 2 + (b ^ near)) for a in range(4) for b in range(2)
    ]
    return lax.ppermute(value, axes, pairs)


def swap_cores(value):
    return lax.ppermute(value, "core", [(0, 1), (1, 0)])


def own_first(terms):
    own = STEPS.index((0, 0))
    return [terms[own]] + terms[:own] + terms[own + 1 :]


def back(step):
    return ((4 - step[0]) % 4, step[1])


def place(first, second, first_here, second_here):
    code = ((first - first_here + 4) % 4) * 2 + (second ^ second_here)
    position = jnp.zeros_like(code)
    for index, (far, near) in enumerate(STEPS):
        position = jnp.where(code == far * 2 + near, index, position)
    return position


def dense_block(blocks, row_index, col_index, tile_total, row_tiles, col_tiles, step_tiles):
    slots, tile, _ = blocks.shape
    height, width = row_tiles * tile, col_tiles * tile
    loads, fill, batch = 4, 32, 8
    share = slots // loads
    size = step_tiles * tile
    stores = width // size // 2

    def kernel(
        rows_ref, cols_ref, total_ref, blocks_ref, own_ref, other_ref, tiles, image, t_sem, s_sem
    ):
        def load(part):
            span = pl.ds(part * share, share)
            return pltpu.make_async_copy(blocks_ref.at[span], tiles.at[span], t_sem.at[part])

        def store(part):
            target = own_ref.at[0, part] if part < stores else other_ref.at[part - stores]
            return pltpu.make_async_copy(
                image.at[:, pl.ds(part * size, size)], target, s_sem.at[part]
            )

        for part in range(loads):
            load(part).start()

        @pl.loop(0, height // fill)
        def _(index):
            image[pl.ds(pl.multiple_of(index * fill, fill), fill)] = jnp.zeros(
                (fill, width), image.dtype
            )

        def put(slot):
            rows = pl.ds(pl.multiple_of(rows_ref[slot] * tile, tile), tile)
            cols = pl.ds(pl.multiple_of(cols_ref[slot] * tile, tile), tile)
            image[rows, cols] = tiles[slot]

        total = total_ref[0]
        for part in range(loads):
            load(part).wait()
            used = jnp.clip(total - part * share, 0, share)

            @pl.loop(0, used // batch)
            def _(group):
                for index in range(batch):
                    put(part * share + group * batch + index)

            @pl.loop(used // batch * batch, used)
            def _(slot):
                put(part * share + slot)

        for part in range(2 * stores):
            store(part).start()
        for part in range(2 * stores):
            store(part).wait()

    smem = pl.BlockSpec(memory_space=pltpu.SMEM)
    return pl.pallas_call(
        kernel,
        out_shape=[
            jax.ShapeDtypeStruct((PLANES, stores, height, size), blocks.dtype),
            jax.ShapeDtypeStruct((stores, height, size), blocks.dtype),
        ],
        in_specs=[smem, smem, smem, ANY],
        out_specs=[ANY, ANY],
        scratch_shapes=[
            pltpu.VMEM((slots, tile, tile), blocks.dtype),
            pltpu.VMEM((height, width), blocks.dtype),
            pltpu.SemaphoreType.DMA((loads,)),
            pltpu.SemaphoreType.DMA((2 * stores,)),
        ],
        compiler_params=pltpu.CompilerParams(vmem_limit_bytes=WIDE_GRANT),
        cost_estimate=pl.CostEstimate(
            flops=0,
            bytes_accessed=2 * (blocks.size + height * width),
            transcendentals=0,
        ),
        name="dense_block",
    )(row_index, col_index, tile_total, blocks)


def products(own, other, panels, first, count, backward, keep):
    joined = not isinstance(panels, list)
    if joined:
        panels = [panels]
        features, depth = panels[0].shape[1:] if backward else panels[0].shape[:0:-1]
        size = depth // (2 * len(STEPS))
    else:
        size = panels[0].shape[1 if backward else 0]
        features = panels[0].shape[0 if backward else 1]
        depth = len(panels) * size
    parts = len(panels)
    half = depth // 2
    pieces = 1 if backward else half // size
    outs = count + (1 if keep else 0)

    def kernel(*refs):
        own_ref, other_ref, p_refs = refs[0], refs[1], refs[2 : 2 + parts]
        o_refs = refs[2 + parts : 2 + parts + outs]
        m_buf, p_buf, o_buf, m_sem, p_sem, o_sem, k_sem = refs[2 + parts + outs :]

        def m_copies(block):
            rows = pl.ds(pl.multiple_of((first + block) * size, size), size)
            for side, source in enumerate((own_ref.at[0], other_ref)):
                for piece in range(pieces):
                    if backward:
                        source_piece = source.at[first + block]
                        target = m_buf.at[block, pl.ds(side * half, half)]
                    else:
                        source_piece = source.at[piece, rows]
                        target = m_buf.at[block, :, pl.ds(side * half + piece * size, size)]
                    sem = m_sem.at[block, side * pieces + piece]
                    yield pltpu.make_async_copy(source_piece, target, sem)

        def p_copy(part):
            if joined:
                return pltpu.make_async_copy(p_refs[0].at[0], p_buf, p_sem.at[0])
            span = pl.ds(part * size, size)
            target = p_buf.at[:, span] if backward else p_buf.at[span]
            return pltpu.make_async_copy(p_refs[part], target, p_sem.at[part])

        def o_copy(block):
            return pltpu.make_async_copy(o_buf.at[block], o_refs[block], o_sem.at[block])

        for part in range(parts):
            p_copy(part).start()
        for copy in m_copies(0):
            copy.start()
        for part in range(parts):
            p_copy(part).wait()
        for block in range(1, count):
            for copy in m_copies(block):
                copy.start()
        if keep:
            kept = pltpu.make_async_copy(p_buf, o_refs[count].at[0], k_sem)
            kept.start()

        @pl.loop(0, count)
        def _(block):
            for copy in m_copies(block):
                copy.wait()
            left, right = (p_buf[...], m_buf[block]) if backward else (m_buf[block], p_buf[...])
            o_buf[block] = jnp.dot(left, right, preferred_element_type=jnp.float32).astype(
                o_buf.dtype
            )
            for index in range(count):

                @pl.when(block == index)
                def _():
                    o_copy(index).start()

        for block in range(count):
            o_copy(block).wait()
        if keep:
            kept.wait()

    shape = (features, size) if backward else (size, features)
    panel = (features, depth) if backward else (depth, features)
    out_shape = [jax.ShapeDtypeStruct(shape, jnp.bfloat16)] * count
    if keep:
        out_shape = out_shape + [jax.ShapeDtypeStruct((PANEL_PLANES,) + panel, jnp.bfloat16)]
    return pl.pallas_call(
        kernel,
        out_shape=out_shape,
        in_specs=[ANY] * (2 + parts),
        out_specs=[ANY] * outs,
        scratch_shapes=[
            pltpu.VMEM((count, depth, size) if backward else (count, size, depth), own.dtype),
            pltpu.VMEM(panel, jnp.bfloat16),
            pltpu.VMEM((count,) + shape, jnp.bfloat16),
            pltpu.SemaphoreType.DMA((count, 2 * pieces)),
            pltpu.SemaphoreType.DMA((parts,)),
            pltpu.SemaphoreType.DMA((count,)),
            pltpu.SemaphoreType.DMA,
        ],
        compiler_params=pltpu.CompilerParams(vmem_limit_bytes=GRANT),
        cost_estimate=pl.CostEstimate(
            flops=2 * count * size * depth * features,
            bytes_accessed=2 * (count * size * (depth + features) + depth * features),
            transcendentals=0,
        ),
        name="backward_products" if backward else "forward_products",
    )(own, other, *panels)


def load_all(sources, targets, sems):
    copies = [
        pltpu.make_async_copy(source, target, sems.at[index])
        for index, (source, target) in enumerate(zip(sources, targets))
    ]
    for copy in copies:
        copy.start()
    return copies


def split_pair(value, lane):
    high = value.astype(jnp.bfloat16)
    low = value - high.astype(jnp.float32)
    return jnp.where(lane == 0, high.astype(jnp.float32), low).astype(jnp.bfloat16)


def node_layer(terms, weight, bias, cotangent):
    nodes, features = cotangent.shape
    parts = len(terms)

    def kernel(*refs):
        sources = refs[: parts + 3]
        output_ref, grads_ref, terms_ref = refs[parts + 3 : parts + 6]
        t_buf, w_buf, b_buf, c_buf, sems = refs[parts + 6 :]
        targets = [t_buf.at[part] for part in range(parts)] + [w_buf, b_buf, c_buf]
        copies = load_all(sources, targets, sems)
        copies[0].wait()
        total = t_buf[0].astype(jnp.float32)
        for part in range(1, parts):
            copies[part].wait()
            total = total + t_buf[part].astype(jnp.float32)
        aggregated = total.astype(jnp.bfloat16)
        for copy in copies[parts:]:
            copy.wait()
        pre = jnp.dot(aggregated, w_buf[...], preferred_element_type=jnp.float32) + b_buf[...]
        gate = jax.nn.sigmoid(pre)
        output_ref[...] = (pre * gate).astype(jnp.bfloat16)
        grad_pre = (
            c_buf[...].astype(jnp.float32) * gate * (1.0 + pre * (1.0 - gate))
        ).astype(jnp.bfloat16)
        grads_ref[...] = lax.dot_general(
            w_buf[...],
            grad_pre,
            (((1,), (1,)), ((), ())),
            preferred_element_type=jnp.float32,
        ).astype(jnp.bfloat16)
        over_nodes = (((0,), (0,)), ((), ()))
        terms_ref[:, :features] = lax.dot_general(
            aggregated, grad_pre, over_nodes, preferred_element_type=jnp.float32
        ).astype(jnp.bfloat16)
        bias_terms = lax.dot_general(
            grad_pre,
            jnp.ones((nodes, LANES), jnp.bfloat16),
            over_nodes,
            preferred_element_type=jnp.float32,
        )
        lane = lax.broadcasted_iota(jnp.int32, bias_terms.shape, 1)
        terms_ref[:, features:] = split_pair(bias_terms, lane)

    return pl.pallas_call(
        kernel,
        out_shape=[
            jax.ShapeDtypeStruct((nodes, features), jnp.bfloat16),
            jax.ShapeDtypeStruct((features, nodes), jnp.bfloat16),
            jax.ShapeDtypeStruct((features, features + LANES), jnp.bfloat16),
        ],
        in_specs=[ANY] * (parts + 3),
        scratch_shapes=[
            pltpu.VMEM((parts, nodes, features), jnp.bfloat16),
            pltpu.VMEM((features, features), jnp.bfloat16),
            pltpu.VMEM((1, features), jnp.float32),
            pltpu.VMEM((nodes, features), jnp.bfloat16),
            pltpu.SemaphoreType.DMA((parts + 3,)),
        ],
        compiler_params=pltpu.CompilerParams(vmem_limit_bytes=GRANT),
        cost_estimate=pl.CostEstimate(
            flops=6 * nodes * features * features,
            bytes_accessed=2 * (12 * nodes * features + 2 * features * features),
            transcendentals=nodes * features,
        ),
        name="node_layer",
    )(*terms, weight, bias.reshape(1, features), cotangent)


def spread_totals(parts, features):
    chips, rows, width = parts.shape

    def kernel(parts_ref, out_ref):
        total = jnp.sum(parts_ref[...].astype(jnp.float32), axis=0)
        pair = total[:, features:]
        lane = lax.broadcasted_iota(jnp.int32, pair.shape, 1)
        bias_total = jnp.broadcast_to(pair[:, :1] + pair[:, 1:2], pair.shape)
        row = jnp.concatenate(
            [total[:, :features].astype(jnp.bfloat16), split_pair(bias_total, lane)], axis=1
        )
        out_ref[...] = jnp.broadcast_to(row[None], (chips, rows, width))

    return pl.pallas_call(
        kernel,
        out_shape=jax.ShapeDtypeStruct((chips, rows, width), jnp.bfloat16),
        compiler_params=pltpu.CompilerParams(vmem_limit_bytes=GRANT),
        cost_estimate=pl.CostEstimate(
            flops=parts.size, bytes_accessed=4 * parts.size, transcendentals=0
        ),
        name="spread_totals",
    )(parts)


def block_sum(terms, finish):
    features, nodes = terms[0].shape
    parts = len(terms)

    def kernel(*refs):
        out_ref, bufs, sems = refs[parts], refs[parts + 1 : -1], refs[-1]
        copies = load_all(refs[:parts], bufs, sems)
        copies[0].wait()
        total = bufs[0][...].astype(jnp.float32)
        for part in range(1, parts):
            copies[part].wait()
            total = total + bufs[part][...].astype(jnp.float32)
        out_ref[...] = total.T.astype(jnp.bfloat16) if finish else total

    shape = (nodes, features) if finish else (features, nodes)
    return pl.pallas_call(
        kernel,
        out_shape=jax.ShapeDtypeStruct(shape, jnp.bfloat16 if finish else jnp.float32),
        in_specs=[ANY] * parts,
        scratch_shapes=[pltpu.VMEM((features, nodes), term.dtype) for term in terms]
        + [pltpu.SemaphoreType.DMA((parts,))],
        compiler_params=pltpu.CompilerParams(vmem_limit_bytes=GRANT),
        cost_estimate=pl.CostEstimate(
            flops=parts * nodes * features,
            bytes_accessed=2 * (parts + 1) * nodes * features,
            transcendentals=0,
        ),
        name="block_sum",
    )(*terms)


def per_device(
    node_features, tile_values, tile_rows, tile_cols, tile_count, weight, bias, cotangent
):
    blocks = tile_values[0]
    tile = blocks.shape[-1]
    local_nodes = node_features.shape[0]
    step_tiles = local_nodes // tile
    row_tiles = step_tiles * lax.axis_size(COL_CHIPS)
    col_tiles = step_tiles * lax.axis_size(ROW_CHIPS + ("core",))
    node_total = local_nodes * lax.axis_size(ALL_CHIPS + ("core",))
    x, yh, core = lax.axis_index("x"), lax.axis_index("yh"), lax.axis_index("core")
    z, yl = lax.axis_index("z"), lax.axis_index("yl")
    steps = len(STEPS)
    features = weight.shape[0]
    chips = lax.axis_size(ALL_CHIPS)

    owner = tile_rows[0] // step_tiles
    row_place = place(owner // 2, owner % 2, z, yl) * step_tiles + tile_rows[0] % step_tiles
    owner = tile_cols[0] // step_tiles
    col_place = place(owner // 4, (owner // 2) % 2, x, yh) + steps * ((owner % 2) ^ core)
    col_place = col_place * step_tiles + tile_cols[0] % step_tiles
    own_half, other_half = dense_block(blocks, row_place, col_place, tile_count[0], row_tiles, col_tiles, step_tiles)

    got = {(0, 0): node_features}
    for step in FIRST_STEPS:
        got[step] = send(node_features, ROW_CHIPS, back(step))
    for step in SEND_STEPS:
        got[step] = send(node_features, ROW_CHIPS, back(step))
    got[2, 1] = send(got[3, 1], ROW_CHIPS, back((3, 0)))
    got[2, 0] = send(got[1, 0], ROW_CHIPS, back((1, 0)))
    swapped = {step: swap_cores(got[step]) for step in got if step not in LATE_STEPS}
    *held, own_half, other_half = lax.optimization_barrier(
        (*(got[step] for step in LATE_STEPS), own_half, other_half)
    )
    got.update(zip(LATE_STEPS, held))
    swapped.update({step: swap_cores(got[step]) for step in LATE_STEPS})
    panels = [got[step] for step in STEPS] + [swapped[step] for step in STEPS]
    their_half = swap_cores(other_half)

    arrived = []
    for first, count in GROUPS:
        partials = products(own_half, other_half, panels, first, count, False, False)
        for partial, step in zip(partials, STEPS[first : first + count]):
            arrived.append(partial if step == (0, 0) else send(partial, COL_CHIPS, step))
    output, grads, terms = node_layer(own_first(arrived), weight, bias, cotangent)

    got = {(0, 0): grads}
    for step in FIRST_STEPS:
        got[step] = send(grads, COL_CHIPS, back(step))
    for step in SEND_STEPS:
        got[step] = send(grads, COL_CHIPS, back(step))
    parts = lax.all_to_all(
        terms.reshape(chips, features // chips, features + LANES),
        ALL_CHIPS, 0, 0, tiled=True,
    )
    got[2, 1] = send(got[3, 1], COL_CHIPS, back((3, 0)))
    got[2, 0] = send(got[1, 0], COL_CHIPS, back((1, 0)))
    swapped = {step: swap_cores(got[step]) for step in got if step not in LATE_STEPS}
    swapped.update({step: swap_cores(got[step]) for step in LATE_STEPS})
    spread = spread_totals(parts, features)
    sums = lax.all_to_all(spread, ALL_CHIPS, 0, 0, tiled=True)

    panels = [got[step] for step in STEPS] + [swapped[step] for step in STEPS]
    arrived = []
    for index, (first, count) in enumerate(GROUPS):
        partials = products(own_half, their_half, panels, first, count, True, index == 0)
        if index == 0:
            *partials, panels = partials
        for partial, step in zip(partials, STEPS[first : first + count]):
            arrived.append(partial if step == (0, 0) else send(partial, ROW_CHIPS, step))

    sums = sums.reshape(features, features + LANES)
    other = swap_cores(sums)
    sums, other = sums.astype(jnp.float32), other.astype(jnp.float32)
    grad_scale = 1.0 / math.sqrt(node_total)
    weight_grad = (sums[:, :features] + other[:, :features]) * grad_scale
    pair, other_pair = sums[:, features : features + 2], other[:, features : features + 2]
    bias_grad = ((pair[:, 0] + pair[:, 1]) + (other_pair[:, 0] + other_pair[:, 1])) * grad_scale

    own = STEPS.index((0, 0))
    total = block_sum([arrived[own]] + arrived[:own], False)
    weight_grad, bias_grad, total = lax.optimization_barrier((weight_grad, bias_grad, total))
    feature_grad = block_sum([total] + arrived[own + 1 :], True)
    return (output, feature_grad, weight_grad, bias_grad)


def solution(mesh):
    mesh = Mesh(mesh.devices.reshape(4, 2, 2, 4, 2), ("x", "yh", "core", "z", "yl"))
    row, col = ("x", "yh", "core"), ("z", "yl")
    return jax.shard_map(
        per_device,
        mesh=mesh,
        in_specs=(
            P(col + row, None),
            P(row, col, None, None),
            P(row, col),
            P(row, col),
            P(row, col),
            P(),
            P(),
            P(row + col, None),
        ),
        out_specs=(P(row + col, None), P(col + row, None), P(), P()),
        check_vma=False,
    )
```

```python
import math

import jax
import jax.numpy as jnp
from jax import lax
from jax.experimental import pallas as pl
from jax.experimental.pallas import tpu as pltpu
from jax.sharding import Mesh, PartitionSpec as P


LANES = 128
STEPS = ((2, 1), (1, 1), (3, 1), (2, 0), (0, 0), (0, 1), (1, 0), (3, 0))
GROUPS = ((0, 4), (4, 4))
FIRST_STEPS = ((3, 1), (1, 0))
SEND_STEPS = ((1, 1), (3, 0), (0, 1))
LATE_STEPS = SEND_STEPS + ((2, 1), (2, 0))
ROW_CHIPS = ("x", "yh")
COL_CHIPS = ("z", "yl")
ALL_CHIPS = ROW_CHIPS + COL_CHIPS
GRANT = 32 * 1024 * 1024
WIDE_GRANT = 58 * 1024 * 1024
PLANES = 5
PANEL_PLANES = 9
ANY = pl.BlockSpec(memory_space=pl.ANY)


def send(value, axes, step):
    far, near = step
    pairs = [
        (a * 2 + b, ((a + far) % 4) * 2 + (b ^ near)) for a in range(4) for b in range(2)
    ]
    return lax.ppermute(value, axes, pairs)


def swap_cores(value):
    return lax.ppermute(value, "core", [(0, 1), (1, 0)])


def own_first(terms):
    own = STEPS.index((0, 0))
    return [terms[own]] + terms[:own] + terms[own + 1 :]


def back(step):
    return ((4 - step[0]) % 4, step[1])


def place(first, second, first_here, second_here):
    code = ((first - first_here + 4) % 4) * 2 + (second ^ second_here)
    position = jnp.zeros_like(code)
    for index, (far, near) in enumerate(STEPS):
        position = jnp.where(code == far * 2 + near, index, position)
    return position


def dense_block(blocks, row_index, col_index, tile_total, row_tiles, col_tiles):
    slots, tile, _ = blocks.shape
    height, width = row_tiles * tile, col_tiles * tile
    loads, stores, fill, batch = 4, 4, 64, 8
    share = slots // loads
    half = width // 2

    def kernel(
        rows_ref, cols_ref, total_ref, blocks_ref, own_ref, other_ref, tiles, image, t_sem, s_sem
    ):
        def load(part):
            span = pl.ds(part * share, share)
            return pltpu.make_async_copy(blocks_ref.at[span], tiles.at[span], t_sem.at[part])

        def store(part):
            span = pl.ds(part // 2 * (height // stores), height // stores)
            target = other_ref.at[span] if part % 2 else own_ref.at[0, span]
            return pltpu.make_async_copy(
                image.at[span, pl.ds(part % 2 * half, half)], target, s_sem.at[part]
            )

        for part in range(loads):
            load(part).start()

        @pl.loop(0, height // fill)
        def _(index):
            image[pl.ds(pl.multiple_of(index * fill, fill), fill)] = jnp.zeros(
                (fill, width), image.dtype
            )

        def put(slot):
            rows = pl.ds(pl.multiple_of(rows_ref[slot] * tile, tile), tile)
            cols = pl.ds(pl.multiple_of(cols_ref[slot] * tile, tile), tile)
            image[rows, cols] = tiles[slot]

        total = total_ref[0]
        for part in range(loads):
            load(part).wait()
            used = jnp.clip(total - part * share, 0, share)

            @pl.loop(0, used // batch)
            def _(group):
                for index in range(batch):
                    put(part * share + group * batch + index)

            @pl.loop(used // batch * batch, used)
            def _(slot):
                put(part * share + slot)

        for part in range(2 * stores):
            store(part).start()
        for part in range(2 * stores):
            store(part).wait()

    smem = pl.BlockSpec(memory_space=pltpu.SMEM)
    return pl.pallas_call(
        kernel,
        out_shape=[
            jax.ShapeDtypeStruct((PLANES, height, half), blocks.dtype),
            jax.ShapeDtypeStruct((height, half), blocks.dtype),
        ],
        in_specs=[smem, smem, smem, ANY],
        out_specs=[ANY, ANY],
        scratch_shapes=[
            pltpu.VMEM((slots, tile, tile), blocks.dtype),
            pltpu.VMEM((height, width), blocks.dtype),
            pltpu.SemaphoreType.DMA((loads,)),
            pltpu.SemaphoreType.DMA((2 * stores,)),
        ],
        compiler_params=pltpu.CompilerParams(vmem_limit_bytes=WIDE_GRANT),
        cost_estimate=pl.CostEstimate(
            flops=0,
            bytes_accessed=2 * (blocks.size + height * width),
            transcendentals=0,
        ),
        name="dense_block",
    )(row_index, col_index, tile_total, blocks)


def products(own, other, panels, first, count, backward, keep):
    joined = not isinstance(panels, list)
    if joined:
        panels = [panels]
        features, depth = panels[0].shape[1:] if backward else panels[0].shape[:0:-1]
        size = depth // (2 * len(STEPS))
    else:
        size = panels[0].shape[1 if backward else 0]
        features = panels[0].shape[0 if backward else 1]
        depth = len(panels) * size
    parts = len(panels)
    half = depth // 2
    outs = count + (1 if keep else 0)

    def kernel(*refs):
        own_ref, other_ref, p_refs = refs[0], refs[1], refs[2 : 2 + parts]
        o_refs = refs[2 + parts : 2 + parts + outs]
        m_buf, p_buf, o_buf, m_sem, p_sem, o_sem, k_sem = refs[2 + parts + outs :]

        def m_copy(block, side):
            span = pl.ds(pl.multiple_of((first + block) * size, size), size)
            source = other_ref if side else own_ref.at[0]
            if backward:
                source, target = source.at[:, span], m_buf.at[block, pl.ds(side * half, half)]
            else:
                source, target = source.at[span], m_buf.at[block, :, pl.ds(side * half, half)]
            return pltpu.make_async_copy(source, target, m_sem.at[block, side])

        def p_copy(part):
            if joined:
                return pltpu.make_async_copy(p_refs[0].at[0], p_buf, p_sem.at[0])
            span = pl.ds(part * size, size)
            target = p_buf.at[:, span] if backward else p_buf.at[span]
            return pltpu.make_async_copy(p_refs[part], target, p_sem.at[part])

        def o_copy(block):
            return pltpu.make_async_copy(o_buf.at[block], o_refs[block], o_sem.at[block])

        for part in range(parts):
            p_copy(part).start()
        for side in range(2):
            m_copy(0, side).start()
        for part in range(parts):
            p_copy(part).wait()
        for block in range(1, count):
            for side in range(2):
                m_copy(block, side).start()
        if keep:
            kept = pltpu.make_async_copy(p_buf, o_refs[count].at[0], k_sem)
            kept.start()

        @pl.loop(0, count)
        def _(block):
            for side in range(2):
                m_copy(block, side).wait()
            left, right = (p_buf[...], m_buf[block]) if backward else (m_buf[block], p_buf[...])
            o_buf[block] = jnp.dot(left, right, preferred_element_type=jnp.float32).astype(
                o_buf.dtype
            )
            for index in range(count):

                @pl.when(block == index)
                def _():
                    o_copy(index).start()

        for block in range(count):
            o_copy(block).wait()
        if keep:
            kept.wait()

    shape = (features, size) if backward else (size, features)
    panel = (features, depth) if backward else (depth, features)
    out_shape = [jax.ShapeDtypeStruct(shape, jnp.bfloat16)] * count
    if keep:
        out_shape = out_shape + [jax.ShapeDtypeStruct((PANEL_PLANES,) + panel, jnp.bfloat16)]
    return pl.pallas_call(
        kernel,
        out_shape=out_shape,
        in_specs=[ANY] * (2 + parts),
        out_specs=[ANY] * outs,
        scratch_shapes=[
            pltpu.VMEM((count, depth, size) if backward else (count, size, depth), own.dtype),
            pltpu.VMEM(panel, jnp.bfloat16),
            pltpu.VMEM((count,) + shape, jnp.bfloat16),
            pltpu.SemaphoreType.DMA((count, 2)),
            pltpu.SemaphoreType.DMA((parts,)),
            pltpu.SemaphoreType.DMA((count,)),
            pltpu.SemaphoreType.DMA,
        ],
        compiler_params=pltpu.CompilerParams(vmem_limit_bytes=GRANT),
        cost_estimate=pl.CostEstimate(
            flops=2 * count * size * depth * features,
            bytes_accessed=2 * (count * size * (depth + features) + depth * features),
            transcendentals=0,
        ),
        name="backward_products" if backward else "forward_products",
    )(own, other, *panels)


def load_all(sources, targets, sems):
    copies = [
        pltpu.make_async_copy(source, target, sems.at[index])
        for index, (source, target) in enumerate(zip(sources, targets))
    ]
    for copy in copies:
        copy.start()
    return copies


def split_pair(value, lane):
    high = value.astype(jnp.bfloat16)
    low = value - high.astype(jnp.float32)
    return jnp.where(lane == 0, high.astype(jnp.float32), low).astype(jnp.bfloat16)


def node_layer(terms, weight, bias, cotangent):
    nodes, features = cotangent.shape
    parts = len(terms)

    def kernel(*refs):
        sources = refs[: parts + 3]
        output_ref, grads_ref, terms_ref = refs[parts + 3 : parts + 6]
        t_buf, w_buf, b_buf, c_buf, sems = refs[parts + 6 :]
        targets = [t_buf.at[part] for part in range(parts)] + [w_buf, b_buf, c_buf]
        copies = load_all(sources, targets, sems)
        copies[0].wait()
        total = t_buf[0].astype(jnp.float32)
        for part in range(1, parts):
            copies[part].wait()
            total = total + t_buf[part].astype(jnp.float32)
        aggregated = total.astype(jnp.bfloat16)
        for copy in copies[parts:]:
            copy.wait()
        pre = jnp.dot(aggregated, w_buf[...], preferred_element_type=jnp.float32) + b_buf[...]
        gate = jax.nn.sigmoid(pre)
        output_ref[...] = (pre * gate).astype(jnp.bfloat16)
        grad_pre = (
            c_buf[...].astype(jnp.float32) * gate * (1.0 + pre * (1.0 - gate))
        ).astype(jnp.bfloat16)
        grads_ref[...] = lax.dot_general(
            w_buf[...],
            grad_pre,
            (((1,), (1,)), ((), ())),
            preferred_element_type=jnp.float32,
        ).astype(jnp.bfloat16)
        over_nodes = (((0,), (0,)), ((), ()))
        terms_ref[:, :features] = lax.dot_general(
            aggregated, grad_pre, over_nodes, preferred_element_type=jnp.float32
        ).astype(jnp.bfloat16)
        bias_terms = lax.dot_general(
            grad_pre,
            jnp.ones((nodes, LANES), jnp.bfloat16),
            over_nodes,
            preferred_element_type=jnp.float32,
        )
        lane = lax.broadcasted_iota(jnp.int32, bias_terms.shape, 1)
        terms_ref[:, features:] = split_pair(bias_terms, lane)

    return pl.pallas_call(
        kernel,
        out_shape=[
            jax.ShapeDtypeStruct((nodes, features), jnp.bfloat16),
            jax.ShapeDtypeStruct((features, nodes), jnp.bfloat16),
            jax.ShapeDtypeStruct((features, features + LANES), jnp.bfloat16),
        ],
        in_specs=[ANY] * (parts + 3),
        scratch_shapes=[
            pltpu.VMEM((parts, nodes, features), jnp.bfloat16),
            pltpu.VMEM((features, features), jnp.bfloat16),
            pltpu.VMEM((1, features), jnp.float32),
            pltpu.VMEM((nodes, features), jnp.bfloat16),
            pltpu.SemaphoreType.DMA((parts + 3,)),
        ],
        compiler_params=pltpu.CompilerParams(vmem_limit_bytes=GRANT),
        cost_estimate=pl.CostEstimate(
            flops=6 * nodes * features * features,
            bytes_accessed=2 * (12 * nodes * features + 2 * features * features),
            transcendentals=nodes * features,
        ),
        name="node_layer",
    )(*terms, weight, bias.reshape(1, features), cotangent)


def spread_totals(parts, features):
    chips, rows, width = parts.shape

    def kernel(parts_ref, out_ref):
        total = jnp.sum(parts_ref[...].astype(jnp.float32), axis=0)
        pair = total[:, features:]
        lane = lax.broadcasted_iota(jnp.int32, pair.shape, 1)
        bias_total = jnp.broadcast_to(pair[:, :1] + pair[:, 1:2], pair.shape)
        row = jnp.concatenate(
            [total[:, :features].astype(jnp.bfloat16), split_pair(bias_total, lane)], axis=1
        )
        out_ref[...] = jnp.broadcast_to(row[None], (chips, rows, width))

    return pl.pallas_call(
        kernel,
        out_shape=jax.ShapeDtypeStruct((chips, rows, width), jnp.bfloat16),
        compiler_params=pltpu.CompilerParams(vmem_limit_bytes=GRANT),
        cost_estimate=pl.CostEstimate(
            flops=parts.size, bytes_accessed=4 * parts.size, transcendentals=0
        ),
        name="spread_totals",
    )(parts)


def block_sum(terms, finish):
    features, nodes = terms[0].shape
    parts = len(terms)

    def kernel(*refs):
        out_ref, bufs, sems = refs[parts], refs[parts + 1 : -1], refs[-1]
        copies = load_all(refs[:parts], bufs, sems)
        copies[0].wait()
        total = bufs[0][...].astype(jnp.float32)
        for part in range(1, parts):
            copies[part].wait()
            total = total + bufs[part][...].astype(jnp.float32)
        out_ref[...] = total.T.astype(jnp.bfloat16) if finish else total

    shape = (nodes, features) if finish else (features, nodes)
    return pl.pallas_call(
        kernel,
        out_shape=jax.ShapeDtypeStruct(shape, jnp.bfloat16 if finish else jnp.float32),
        in_specs=[ANY] * parts,
        scratch_shapes=[pltpu.VMEM((features, nodes), term.dtype) for term in terms]
        + [pltpu.SemaphoreType.DMA((parts,))],
        compiler_params=pltpu.CompilerParams(vmem_limit_bytes=GRANT),
        cost_estimate=pl.CostEstimate(
            flops=parts * nodes * features,
            bytes_accessed=2 * (parts + 1) * nodes * features,
            transcendentals=0,
        ),
        name="block_sum",
    )(*terms)


def per_device(
    node_features, tile_values, tile_rows, tile_cols, tile_count, weight, bias, cotangent
):
    blocks = tile_values[0]
    tile = blocks.shape[-1]
    local_nodes = node_features.shape[0]
    step_tiles = local_nodes // tile
    row_tiles = step_tiles * lax.axis_size(COL_CHIPS)
    col_tiles = step_tiles * lax.axis_size(ROW_CHIPS + ("core",))
    node_total = local_nodes * lax.axis_size(ALL_CHIPS + ("core",))
    x, yh, core = lax.axis_index("x"), lax.axis_index("yh"), lax.axis_index("core")
    z, yl = lax.axis_index("z"), lax.axis_index("yl")
    steps = len(STEPS)
    features = weight.shape[0]
    chips = lax.axis_size(ALL_CHIPS)

    owner = tile_rows[0] // step_tiles
    row_place = place(owner // 2, owner % 2, z, yl) * step_tiles + tile_rows[0] % step_tiles
    owner = tile_cols[0] // step_tiles
    col_place = place(owner // 4, (owner // 2) % 2, x, yh) + steps * ((owner % 2) ^ core)
    col_place = col_place * step_tiles + tile_cols[0] % step_tiles
    own_half, other_half = dense_block(blocks, row_place, col_place, tile_count[0], row_tiles, col_tiles)

    got = {(0, 0): node_features}
    for step in FIRST_STEPS:
        got[step] = send(node_features, ROW_CHIPS, back(step))
    for step in SEND_STEPS:
        got[step] = send(node_features, ROW_CHIPS, back(step))
    got[2, 1] = send(got[3, 1], ROW_CHIPS, back((3, 0)))
    got[2, 0] = send(got[1, 0], ROW_CHIPS, back((1, 0)))
    swapped = {step: swap_cores(got[step]) for step in got if step not in LATE_STEPS}
    *held, own_half, other_half = lax.optimization_barrier(
        (*(got[step] for step in LATE_STEPS), own_half, other_half)
    )
    got.update(zip(LATE_STEPS, held))
    swapped.update({step: swap_cores(got[step]) for step in LATE_STEPS})
    panels = [got[step] for step in STEPS] + [swapped[step] for step in STEPS]
    their_half = swap_cores(other_half)

    arrived = []
    for first, count in GROUPS:
        partials = products(own_half, other_half, panels, first, count, False, False)
        for partial, step in zip(partials, STEPS[first : first + count]):
            arrived.append(partial if step == (0, 0) else send(partial, COL_CHIPS, step))
    output, grads, terms = node_layer(own_first(arrived), weight, bias, cotangent)

    got = {(0, 0): grads}
    for step in FIRST_STEPS:
        got[step] = send(grads, COL_CHIPS, back(step))
    for step in SEND_STEPS:
        got[step] = send(grads, COL_CHIPS, back(step))
    parts = lax.all_to_all(
        terms.reshape(chips, features // chips, features + LANES),
        ALL_CHIPS, 0, 0, tiled=True,
    )
    got[2, 1] = send(got[3, 1], COL_CHIPS, back((3, 0)))
    got[2, 0] = send(got[1, 0], COL_CHIPS, back((1, 0)))
    swapped = {step: swap_cores(got[step]) for step in got if step not in LATE_STEPS}
    swapped.update({step: swap_cores(got[step]) for step in LATE_STEPS})
    spread = spread_totals(parts, features)
    sums = lax.all_to_all(spread, ALL_CHIPS, 0, 0, tiled=True)

    panels = [got[step] for step in STEPS] + [swapped[step] for step in STEPS]
    arrived = []
    for index, (first, count) in enumerate(GROUPS):
        partials = products(own_half, their_half, panels, first, count, True, index == 0)
        if index == 0:
            *partials, panels = partials
        for partial, step in zip(partials, STEPS[first : first + count]):
            arrived.append(partial if step == (0, 0) else send(partial, ROW_CHIPS, step))

    sums = sums.reshape(features, features + LANES)
    other = swap_cores(sums)
    sums, other = sums.astype(jnp.float32), other.astype(jnp.float32)
    grad_scale = 1.0 / math.sqrt(node_total)
    weight_grad = (sums[:, :features] + other[:, :features]) * grad_scale
    pair, other_pair = sums[:, features : features + 2], other[:, features : features + 2]
    bias_grad = ((pair[:, 0] + pair[:, 1]) + (other_pair[:, 0] + other_pair[:, 1])) * grad_scale

    own = STEPS.index((0, 0))
    total = block_sum([arrived[own]] + arrived[:own], False)
    weight_grad, bias_grad, total = lax.optimization_barrier((weight_grad, bias_grad, total))
    feature_grad = block_sum([total] + arrived[own + 1 :], True)
    return (output, feature_grad, weight_grad, bias_grad)


def solution(mesh):
    mesh = Mesh(mesh.devices.reshape(4, 2, 2, 4, 2), ("x", "yh", "core", "z", "yl"))
    row, col = ("x", "yh", "core"), ("z", "yl")
    return jax.shard_map(
        per_device,
        mesh=mesh,
        in_specs=(
            P(col + row, None),
            P(row, col, None, None),
            P(row, col),
            P(row, col),
            P(row, col),
            P(),
            P(),
            P(row + col, None),
        ),
        out_specs=(P(row + col, None), P(col + row, None), P(), P()),
        check_vma=False,
    )
```
